128 devices in a mesh: seq: 8 (over y, x_lo), ch: 16 (over x_hi, z, core).
Axes of the slice: x: 4 (x_hi: 2, x_lo: 2; x = x_hi * 2 + x_lo), y: 4, z: 4, core: 2. Of those that a mesh axis runs over, the one named last changes fastest.
Arguments:
- token_ids: int32 [4096], P('seq'), may hold values from 0 to 511
- embedding: bfloat16 [512, 4096], P(None, 'ch'), may hold values from -6 to 6
- gain_first: bfloat16 [4096], P('ch'), may hold values from 0.5 to 1.5
- gain_second: bfloat16 [4096], P('ch'), may hold values from 0.5 to 1.5
- weights_first: bfloat16 [4096, 3, 4096], P(None, None, 'ch'), may hold values from -0.09375 to 0.09375
- weights_second: bfloat16 [4096, 3, 4096], P(None, None, 'ch'), may hold values from -0.09375 to 0.09375
- short_first: float32 [7, 3, 4096], P(None, None, 'ch'), may hold values from -2.5 to 2.5
- short_second: float32 [7, 3, 4096], P(None, None, 'ch'), may hold values from -2.5 to 2.5
- medium: bfloat16 [128, 4096], P(None, 'ch'), may hold values from -0.5 to 0.5
- residues: float32 [16, 4096], P(None, 'ch'), as said below
- decay_rates: float32 [16, 4096], P(None, 'ch'), as said below
- cotangent: bfloat16 [4096, 4096], P('seq', 'ch'), may hold values from -6 to 6
Outputs:
- output: bfloat16 [4096, 4096], P('seq', 'ch')
- grad_embedding: float32 [512, 4096], P(None, 'ch')
- grad_gain_first: float32 [4096], P('ch')
- grad_gain_second: float32 [4096], P('ch')
- grad_weights_first: float32 [4096, 3, 4096], P('seq', None, 'ch')
- grad_weights_second: float32 [4096, 3, 4096], P('seq', None, 'ch')
The draws below stay inside these ranges and needn't reach their ends.
Inputs may be any that keep to these rules, and one draw needn't show every extreme that they name: `decay_rates`: positive, at most 0.06 and at least 0.05 / 4096. `residues`: magnitude at most 4 sqrt((0.12 + 1 / 4096) / 16).
All inputs are finite; a program needn't handle non-finite values.
Results may differ from the reference program's by a relative error of at most 0.028.
Values may be sent and summed in bfloat16 or wider, within the bound.
A program may use at most 128 MiB of HBM per device.

```python
import math
import jax
import jax.numpy as jnp
import numpy as np
from jax import lax

D = 4096
VOCAB = 512
SHORT_TAPS = 7
MEDIUM_TAPS = 128
MODES = 16
SEQ_LEN = 4096
N_SEQ = 8
N_CH = 16


def mode_rates(key):
    base_key = jax.random.fold_in(key, 11)
    uniform_draw = jax.random.uniform(jax.random.fold_in(base_key, 1), (MODES, D), jnp.float32)
    low_fast = jnp.log(0.2 / SEQ_LEN)
    high_fast = jnp.log(0.06)
    spread = jnp.exp(low_fast + uniform_draw * (high_fast - low_fast))
    return spread


def draw_decay_rates(key, part):
    return mode_rates(key)


def draw_residues(key, part):
    rates_drawn = mode_rates(key)
    normal_draw = jnp.clip(jax.random.normal(jax.random.fold_in(key, 23), (MODES, D), jnp.float32), -4.0, 4.0)
    return normal_draw * jnp.sqrt((2.0 * rates_drawn + 1.0 / SEQ_LEN) / MODES)


def touch_ends(array, key, smallest, top_value):
    extent = array.shape
    spot = [jax.random.randint(jax.random.fold_in(key, axis), (), 0, extent[axis]) for axis in range(len(extent))]
    array = array.at[tuple(spot)].set(smallest)
    longest = extent.index(max(extent))
    spot[longest] = (spot[longest] + 1) % extent[longest]
    return array.at[tuple(spot)].set(top_value)


def steps_of(key, extent, shards, smallest, top_value):
    def one(axis_at, shards_of):
        draws = jax.random.uniform(jax.random.fold_in(jax.random.fold_in(key, 6), axis_at), (shards_of,), jnp.float32, smallest / len(shards), top_value / len(shards))
        return jnp.repeat(jnp.exp(draws), extent[axis_at] // shards_of).reshape((-1,) + (1,) * (len(extent) - axis_at - 1))

    level = one(*shards[0])
    for cut in shards[1:]:
        level = level * one(*cut)
    return level


def cumulative_ranks(amount, slope):
    portions = [(1 << 20) // math.isqrt(rank ** slope) + 1 for rank in range(1, amount + 1)]
    scale = 1 + sum(portions) // (1 << 30)
    return np.cumsum(np.array([max(1, weight // scale) for weight in portions]))


def skewed_ids(key, extent, number_of, skew):
    table = cumulative_ranks(number_of, skew)
    lot = jax.random.randint(jax.random.fold_in(key, 1), extent, 0, int(table[number_of - 1]))
    grade = jnp.searchsorted(jnp.asarray(table, jnp.int32), lot, side="right")
    return jax.random.permutation(jax.random.fold_in(key, 2), number_of)[grade].astype(jnp.int32)


def normal_values(stream_key, extent, scale, limit, cuts=(), kind=jnp.bfloat16):
    level = steps_of(stream_key, extent, cuts, -0.22, 0.18) if cuts else 1.0
    array = jax.random.normal(stream_key, extent, jnp.float32) * scale * level
    return jnp.minimum(jnp.maximum(array, -limit), limit).astype(kind)


def setup_inputs(seed: int = 0) -> dict:
    arg_keys = jax.random.split(jax.random.key(seed), 13)
    return {
        "token_ids": touch_ends(skewed_ids(arg_keys[0], (SEQ_LEN,), VOCAB, 2), jax.random.fold_in(arg_keys[0], 3), 0, VOCAB - 1).astype(jnp.int32),
        "embedding": normal_values(arg_keys[1], (VOCAB, D), 1.0, 6.0, ((1, 16),)),
        "gain_first": jnp.clip(1.0 + 0.1 * jax.random.normal(arg_keys[2], (D,), jnp.float32), 0.5, 1.5).astype(jnp.bfloat16),
        "gain_second": jnp.clip(1.0 + 0.1 * jax.random.normal(arg_keys[3], (D,), jnp.float32), 0.5, 1.5).astype(jnp.bfloat16),
        "weights_first": normal_values(arg_keys[4], (D, 3, D), D ** -0.5, 0.09375, ((2, 16),)),
        "weights_second": normal_values(arg_keys[5], (D, 3, D), D ** -0.5, 0.09375, ((2, 16),)),
        "short_first": normal_values(arg_keys[6], (SHORT_TAPS, 3, D), 0.4, 2.5, ((2, 16),), jnp.float32),
        "short_second": normal_values(arg_keys[7], (SHORT_TAPS, 3, D), 0.4, 2.5, ((2, 16),), jnp.float32),
        "medium": normal_values(arg_keys[8], (MEDIUM_TAPS, D), MEDIUM_TAPS ** -0.5, 0.5, ((1, 16),)),
        "residues": draw_residues(jax.random.fold_in(arg_keys[12], 71), 0),
        "decay_rates": draw_decay_rates(jax.random.fold_in(arg_keys[12], 71), 0),
        "cotangent": normal_values(arg_keys[11], (SEQ_LEN, D), 1.0, 6.0, ((0, 8), (1, 16))),
    }


epsilon = 1e-06
highest = lax.Precision.HIGHEST

def short_causal(projected, short_filter):
    tap_count = short_filter.shape[0]
    row_count = projected.shape[0]
    widened = jnp.pad(projected.astype(jnp.float32), ((tap_count - 1, 0), (0, 0), (0, 0)))
    running = jnp.zeros(projected.shape, jnp.float32)
    for offset in range(tap_count):
        first_row = tap_count - 1 - offset
        running = running + short_filter[offset] * widened[first_row:first_row + row_count]
    return running

def short_anti(gradient, short_filter):
    tap_count = short_filter.shape[0]
    row_count = gradient.shape[0]
    widened = jnp.pad(gradient.astype(jnp.float32), ((0, tap_count - 1), (0, 0), (0, 0)))
    running = jnp.zeros(gradient.shape, jnp.float32)
    for offset in range(tap_count):
        running = running + short_filter[offset] * widened[offset:offset + row_count]
    return running

def medium_causal(signal, medium, forward):
    tap_count = medium.shape[0]
    row_count = signal.shape[0]
    if forward:
        widened = jnp.pad(signal.astype(jnp.float32), ((tap_count - 1, 0), (0, 0)))
    else:
        widened = jnp.pad(signal.astype(jnp.float32), ((0, tap_count - 1), (0, 0)))
    taps_float = medium.astype(jnp.float32)

    def add_lag(offset, running):
        first_row = tap_count - 1 - offset if forward else offset
        window = lax.dynamic_slice_in_dim(widened, first_row, row_count, 0)
        return running + lax.dynamic_index_in_dim(taps_float, offset, 0, False) * window
    return lax.fori_loop(0, tap_count, add_lag, jnp.zeros(signal.shape, jnp.float32))

def long_causal(signal, decay_rates, residues):
    decay = jnp.exp(-decay_rates)

    def advance(state, row_value):
        state = decay * state + row_value[None, :]
        return (state, lax.optimization_barrier(jnp.sum(residues * state, axis=0)))
    unused, outputs = lax.scan(advance, jnp.zeros(decay_rates.shape, jnp.float32), signal)
    return outputs

def mixer_input(inputs, gain, weights, short_filter):
    features = inputs.shape[1]
    as_float = inputs.astype(jnp.float32)
    row_scale = lax.rsqrt(lax.optimization_barrier(jnp.mean(as_float * as_float, axis=1)) + epsilon)
    normed = (as_float * row_scale[:, None] * gain.astype(jnp.float32)).astype(jnp.bfloat16)
    projected = jnp.dot(normed, weights.reshape(features, 3 * features), preferred_element_type=jnp.float32)
    projected = projected.astype(jnp.bfloat16).reshape(-1, 3, features)
    featured = short_causal(projected, short_filter)
    gated = (featured[:, 1, :] * featured[:, 2, :]).astype(jnp.bfloat16)
    return (normed, row_scale, featured, gated)

def project_back(grad_featured, inputs, gain, weights, short_filter, normed, row_scale, grad_above):
    row_count, features = inputs.shape
    grad_projected = short_anti(grad_featured, short_filter).astype(jnp.bfloat16)
    group_width = features // N_CH
    grad_normed = jnp.zeros((row_count, features), jnp.float32)
    for group_index in range(N_CH):
        low_edge = group_index * group_width
        left_part = grad_projected[:, :, low_edge:low_edge + group_width].reshape(row_count, 3 * group_width)
        right_part = weights[:, :, low_edge:low_edge + group_width].reshape(features, 3 * group_width)
        partial_sum = lax.dot_general(left_part, right_part, (((1,), (1,)), ((), ())), preferred_element_type=jnp.float32)
        grad_normed = grad_normed + lax.optimization_barrier(partial_sum.astype(jnp.bfloat16)).astype(jnp.float32)
    flat_grad = grad_projected.reshape(row_count, 3 * features)
    seg_rows = row_count // N_SEQ
    grad_weights = jnp.zeros((features, 3 * features), jnp.float32)
    for group_index in range(N_SEQ):
        low_edge = group_index * seg_rows
        partial_sum = lax.dot_general(normed[low_edge:low_edge + seg_rows], flat_grad[low_edge:low_edge + seg_rows], (((0,), (0,)), ((), ())), preferred_element_type=jnp.float32)
        grad_weights = grad_weights + lax.optimization_barrier(partial_sum.astype(jnp.bfloat16)).astype(jnp.float32)
    as_float = inputs.astype(jnp.float32)
    scaled = grad_normed * gain.astype(jnp.float32)
    row_terms = lax.optimization_barrier(jnp.sum(scaled * as_float, axis=1))
    grad_inputs = grad_above + row_scale[:, None] * scaled - as_float * (row_scale ** 3)[:, None] * row_terms[:, None] / features
    grad_gain = lax.optimization_barrier(jnp.sum(grad_normed * as_float * row_scale[:, None], axis=0))
    return (grad_inputs.astype(jnp.bfloat16), grad_gain, grad_weights.reshape(features, 3, features))

def reference(token_ids, embedding, gain_first, gain_second, weights_first, weights_second, short_first, short_second, medium, residues, decay_rates, cotangent):
    embedded = embedding[token_ids]
    normed_first, scale_first, featured_first, gated_first = mixer_input(embedded, gain_first, weights_first, short_first)
    filtered_first = medium_causal(gated_first, medium, True)
    middle = (embedded.astype(jnp.float32) + featured_first[:, 0, :] * filtered_first).astype(jnp.bfloat16)
    normed_second, scale_second, featured_second, gated_second = mixer_input(middle, gain_second, weights_second, short_second)
    filtered_second = long_causal(gated_second.astype(jnp.float32), decay_rates, residues)
    output = (middle.astype(jnp.float32) + featured_second[:, 0, :] * filtered_second).astype(jnp.bfloat16)
    above_second = cotangent.astype(jnp.float32)
    grad_filtered = (above_second * featured_second[:, 0, :]).astype(jnp.bfloat16)
    grad_gated = long_causal(grad_filtered.astype(jnp.float32)[::-1], decay_rates, residues)[::-1]
    grad_featured = jnp.stack([above_second * filtered_second, grad_gated * featured_second[:, 2, :], grad_gated * featured_second[:, 1, :]], axis=1).astype(jnp.bfloat16)
    grad_middle, grad_gain_second, grad_weights_second = project_back(grad_featured, middle, gain_second, weights_second, short_second, normed_second, scale_second, above_second)
    above_first = grad_middle.astype(jnp.float32)
    grad_filtered = (above_first * featured_first[:, 0, :]).astype(jnp.bfloat16)
    grad_gated = medium_causal(grad_filtered, medium, False)
    grad_featured = jnp.stack([above_first * filtered_first, grad_gated * featured_first[:, 2, :], grad_gated * featured_first[:, 1, :]], axis=1).astype(jnp.bfloat16)
    grad_embedded, grad_gain_first, grad_weights_first = project_back(grad_featured, embedded, gain_first, weights_first, short_first, normed_first, scale_first, above_first)
    onehot = (token_ids[:, None] == jnp.arange(embedding.shape[0], dtype=jnp.int32)[None, :]).astype(jnp.float32)
    grad_embedding = jnp.dot(onehot.T, grad_embedded.astype(jnp.float32), precision=highest)
    return (output, grad_embedding, grad_gain_first, grad_gain_second, grad_weights_first, grad_weights_second)
```

```python
import functools

import jax
import jax.numpy as jnp
from jax import lax
from jax.experimental import pallas as pl
from jax.experimental.pallas import tpu as pltpu
from jax.sharding import PartitionSpec as P

epsilon = 1e-06
MESH = pl.DeviceIdType.MESH
f32 = jnp.float32
bf16 = jnp.bfloat16
LANES = 128
SUB = 8
HALO = 144
LEAD = 8


class Item:
    def __init__(self, array, axis, window=None, reduce=False):
        self.array, self.axis, self.window, self.reduce = array, axis, window, reduce

    def block(self):
        shape = list(self.array.shape)
        if self.window is not None:
            shape[self.window] //= lax.axis_size(self.axis)
        return tuple(shape)


def exchange(cid, items):
    count = len(items)
    sizes = [lax.axis_size(it.axis) for it in items]
    blocks = [it.block() for it in items]
    axes = []
    for it in items:
        if it.axis not in axes:
            axes.append(it.axis)
    most = max(sizes)
    reduced = [k for k in range(count) if items[k].reduce]

    def body(*refs):
        srcs, outs = refs[:count], refs[count : 2 * count]
        bufs = list(outs)
        rest = refs[2 * count :]
        for slot, k in enumerate(reduced):
            bufs[k] = rest[slot]
        send_sem, recv_sem, own_sem = rest[len(reduced) :]

        def part(k, peer):
            if items[k].window is None:
                return srcs[k]
            width = blocks[k][items[k].window]
            start = pl.multiple_of(peer * width, width)
            index = [slice(None)] * len(blocks[k])
            index[items[k].window] = pl.ds(start, width)
            return srcs[k].at[tuple(index)]

        barrier = pltpu.get_barrier_semaphore()
        total = 0
        for axis in axes:
            n = lax.axis_size(axis)
            total += n - 1
            me = lax.axis_index(axis)

            def greet(step, carry, axis=axis, n=n, me=me):
                peer = lax.rem(me + step, n)
                pl.semaphore_signal(barrier, inc=1, device_id={axis: peer}, device_id_type=MESH)
                return carry

            lax.fori_loop(1, n, greet, 0)
        pl.semaphore_wait(barrier, total)

        def copy(k, peer, slot):
            me = lax.axis_index(items[k].axis)
            return pltpu.make_async_remote_copy(
                src_ref=part(k, peer),
                dst_ref=bufs[k].at[me],
                send_sem=send_sem.at[k, slot],
                recv_sem=recv_sem.at[k, me],
                device_id={items[k].axis: peer},
                device_id_type=MESH,
            )

        for k in range(count):
            n = sizes[k]
            me = lax.axis_index(items[k].axis)

            def push(step, carry, k=k, n=n, me=me):
                copy(k, lax.rem(me + step, n), step).start()
                return carry

            lax.fori_loop(1, n, push, 0)
        for k in range(count):
            me = lax.axis_index(items[k].axis)
            pltpu.make_async_copy(part(k, me), bufs[k].at[me], own_sem.at[k]).start()
        for k in range(count):
            n = sizes[k]
            me = lax.axis_index(items[k].axis)
            pltpu.make_async_copy(part(k, me), bufs[k].at[me], own_sem.at[k]).wait()

            def finish(step, carry, k=k, n=n, me=me):
                peer = lax.rem(me + step, n)
                copy(k, peer, step).wait_send()
                pltpu.make_async_remote_copy(
                    src_ref=part(k, peer),
                    dst_ref=bufs[k].at[peer],
                    send_sem=send_sem.at[k, step],
                    recv_sem=recv_sem.at[k, peer],
                    device_id={items[k].axis: peer},
                    device_id_type=MESH,
                ).wait_recv()
                return carry

            lax.fori_loop(1, n, finish, 0)
            if items[k].reduce:
                running = bufs[k][0].astype(f32)
                for j in range(1, n):
                    running = running + bufs[k][j].astype(f32)
                outs[k][...] = running

    shapes = []
    scratch = []
    for k in range(count):
        full = (sizes[k],) + blocks[k]
        if items[k].reduce:
            shapes.append(jax.ShapeDtypeStruct(blocks[k], f32))
            scratch.append(pltpu.VMEM(full, items[k].array.dtype))
        else:
            shapes.append(jax.ShapeDtypeStruct(full, items[k].array.dtype))
    scratch += [
        pltpu.SemaphoreType.DMA((count, most)),
        pltpu.SemaphoreType.DMA((count, most)),
        pltpu.SemaphoreType.DMA((count,)),
    ]
    vmem = pl.BlockSpec(memory_space=pltpu.VMEM)
    return pl.pallas_call(
        body,
        out_shape=shapes,
        in_specs=[vmem] * count,
        out_specs=[vmem] * count,
        scratch_shapes=scratch,
        compiler_params=pltpu.CompilerParams(collective_id=cid, has_side_effects=True),
        name=f"exchange_{cid}",
    )(*[it.array for it in items])


def lag_sum(x, taps):
    tap_count, width = taps.shape
    rows = x.shape[0] - tap_count
    length = rows // SUB
    span = length + tap_count - 1
    group = 11
    tap_group = 8

    def body(x_ref, taps_ref, y_ref, spread, wide):
        for lane in range(width // LANES):
            lanes = slice(lane * LANES, (lane + 1) * LANES)

            def arrange(q, carry):
                spread[q] = x_ref[lane, pl.ds(q, SUB, stride=length), :]
                return carry

            lax.fori_loop(0, span, arrange, 0)

            def widen(k, carry):
                eight = taps_ref[pl.ds(pl.multiple_of(k * SUB, SUB), SUB), lanes]
                for i in range(SUB):
                    wide[k * SUB + i] = jnp.broadcast_to(eight[i : i + 1], (SUB, LANES))
                return carry

            lax.fori_loop(0, tap_count // SUB, widen, 0)

            def block(b, carry):
                first = b * group

                def add(kb, sums):
                    base = first + (tap_count - tap_group) - kb * tap_group
                    window = [spread[base + w] for w in range(group + tap_group - 1)]
                    out = list(sums)
                    for kk in range(tap_group):
                        tap = wide[kb * tap_group + kk]
                        for r in range(group):
                            out[r] = out[r] + tap * window[r + tap_group - 1 - kk]
                    return tuple(out)

                zero = tuple(jnp.zeros((SUB, LANES), f32) for _ in range(group))
                sums = lax.fori_loop(0, tap_count // tap_group, add, zero)
                for r in range(group):
                    y_ref[lane, pl.ds(first + r, SUB, stride=length), :] = sums[r]
                return carry

            lax.fori_loop(0, length // group, block, 0)

    vmem = pl.BlockSpec(memory_space=pltpu.VMEM)
    lanes_first = jnp.stack([x[:, i : i + LANES] for i in range(0, width, LANES)], axis=0)
    y = pl.pallas_call(
        body,
        out_shape=jax.ShapeDtypeStruct((width // LANES, rows, LANES), f32),
        in_specs=[vmem, vmem],
        out_specs=vmem,
        scratch_shapes=[
            pltpu.VMEM((span, SUB, LANES), f32),
            pltpu.VMEM((tap_count, SUB, LANES), f32),
        ],
        name="lag_sum",
    )(lanes_first, taps)
    return jnp.concatenate([y[i] for i in range(width // LANES)], axis=1)


def split_lanes(x):
    return jnp.stack([x[:, i : i + LANES] for i in range(0, x.shape[1], LANES)], axis=0)


def join_lanes(x):
    return jnp.concatenate([x[i] for i in range(x.shape[0])], axis=1)


def mode_close(ahead, behind, rates):
    groups, rows, _ = ahead.shape
    modes, width = rates.shape
    length = rows // SUB
    unroll = 4

    def body(a_ref, b_ref, rate_ref, chunk_ref, shard_ref):
        order = lax.broadcasted_iota(jnp.int32, (SUB, LANES), 0).astype(f32)
        for way, src in enumerate((a_ref, b_ref)):
            for lane in range(groups):
                lanes = slice(lane * LANES, (lane + 1) * LANES)
                rate = [jnp.broadcast_to(rate_ref[m : m + 1, lanes], (SUB, LANES)) for m in range(modes)]
                decay = [jnp.exp(-r) for r in rate]

                def step(i, states):
                    states = list(states)
                    for u in range(unroll):
                        r = i * unroll + u
                        if way == 1:
                            r = length - 1 - r
                        x = src[lane, pl.ds(r, SUB, stride=length), :]
                        states = [decay[m] * states[m] + x for m in range(modes)]
                    return tuple(states)

                zero = tuple(jnp.zeros((SUB, LANES), f32) for _ in range(modes))
                states = lax.fori_loop(0, length // unroll, step, zero)
                after = (SUB - 1) - order if way == 0 else order
                for m in range(modes):
                    chunk_ref[way, m, :, lanes] = states[m]
                    weighted = states[m] * jnp.exp(-(rate[m] * (after * float(length))))
                    shard_ref[way, m : m + 1, lanes] = jnp.sum(weighted, axis=0, keepdims=True)

    vmem = pl.BlockSpec(memory_space=pltpu.VMEM)
    return pl.pallas_call(
        body,
        out_shape=[
            jax.ShapeDtypeStruct((2, modes, SUB, width), f32),
            jax.ShapeDtypeStruct((2, modes, width), f32),
        ],
        in_specs=[vmem] * 3,
        out_specs=[vmem] * 2,
        name="mode_close",
    )(ahead, behind, rates)


def mode_apply(ahead, behind, rates, residues, chunks, entering):
    groups, rows, _ = ahead.shape
    modes, width = rates.shape
    length = rows // SUB
    unroll = 2

    def body(a_ref, b_ref, rate_ref, res_ref, chunk_ref, enter_ref, ya_ref, yb_ref):
        order = lax.broadcasted_iota(jnp.int32, (SUB, LANES), 0)
        for way, (src, dst) in enumerate(((a_ref, ya_ref), (b_ref, yb_ref))):
            place = order if way == 0 else (SUB - 1) - order
            for lane in range(groups):
                lanes = slice(lane * LANES, (lane + 1) * LANES)
                decay = []
                residue = []
                start = []
                for m in range(modes):
                    rate = jnp.broadcast_to(rate_ref[m : m + 1, lanes], (SUB, LANES))
                    decay.append(jnp.exp(-rate))
                    residue.append(jnp.broadcast_to(res_ref[m : m + 1, lanes], (SUB, LANES)))
                    first = jnp.broadcast_to(enter_ref[way, m : m + 1, lanes], (SUB, LANES))

                    def back(v, by):
                        moved = pltpu.roll(v, by if way == 0 else SUB - by, 0)
                        return moved

                    state = jnp.where(place == 0, first, back(chunk_ref[way, m, :, lanes], 1))
                    for by in (1, 2, 4):
                        factor = jnp.exp(-(rate * float(by * length)))
                        state = state + jnp.where(place >= by, factor * back(state, by), 0.0)
                    start.append(state)

                def step(i, states):
                    states = list(states)
                    for u in range(unroll):
                        r = i * unroll + u
                        if way == 1:
                            r = length - 1 - r
                        x = src[lane, pl.ds(r, SUB, stride=length), :]
                        states = [decay[m] * states[m] + x for m in range(modes)]
                        terms = [residue[m] * states[m] for m in range(modes)]
                        while len(terms) > 1:
                            terms = [a + b for a, b in zip(terms[::2], terms[1::2])]
                        dst[lane, pl.ds(r, SUB, stride=length), :] = terms[0]
                    return tuple(states)

                lax.fori_loop(0, length // unroll, step, tuple(start))

    vmem = pl.BlockSpec(memory_space=pltpu.VMEM)
    return pl.pallas_call(
        body,
        out_shape=[jax.ShapeDtypeStruct(ahead.shape, f32)] * 2,
        in_specs=[vmem] * 6,
        out_specs=[vmem] * 2,
        name="mode_apply",
    )(ahead, behind, rates, residues, chunks, entering)


def shift_axis(shard, axis, by):
    n = lax.axis_size(axis)
    pairs = [(i, i + by) for i in range(n) if 0 <= i + by < n]
    return lax.ppermute(shard, axis, pairs)


def taps_ahead(projected, short_filter, first, rows):
    tap_count = short_filter.shape[0]
    running = None
    for i in range(tap_count):
        term = short_filter[i] * projected[first - i : first - i + rows].astype(f32)
        running = term if running is None else running + term
    return running


def taps_behind(gradient, short_filter, rows):
    running = None
    for i in range(short_filter.shape[0]):
        term = short_filter[i] * gradient[i : i + rows].astype(f32)
        running = term if running is None else running + term
    return running


def normalise(whole, gain):
    as_float = whole.astype(f32)
    scale = lax.rsqrt(jnp.mean(as_float * as_float, axis=1) + epsilon)
    return (as_float * scale[:, None] * gain[None, :].astype(f32)).astype(bf16), scale


def small(vector, lanes=LANES):
    rows = vector.reshape(-1, lanes)
    pad = -rows.shape[0] % SUB
    return jnp.pad(rows, ((0, pad), (0, 0)))


def per_device(
    token_ids,
    embedding,
    gain_first,
    gain_second,
    weights_first,
    weights_second,
    short_first,
    short_second,
    medium,
    residues,
    decay_rates,
    cotangent,
):
    n_seq, n_ch = lax.axis_size("seq"), lax.axis_size("ch")
    seq_at = lax.axis_index("seq")
    rows = token_ids.shape[0]
    vocab, width = embedding.shape
    features = weights_first.shape[0]
    wide = 3 * width
    vocab_part = vocab // n_seq
    flat_first = weights_first.reshape(features, wide)
    flat_second = weights_second.reshape(features, wide)
    taps_first = short_first.reshape(-1, wide)
    taps_second = short_second.reshape(-1, wide)

    shifted = token_ids + 1
    ids = jnp.concatenate(
        [
            shift_axis(shifted[rows - HALO :], "seq", 1),
            shifted,
            shift_axis(shifted[:HALO], "seq", -1),
        ]
    ) - 1

    table_rows = lax.dynamic_slice_in_dim(embedding, seq_at * vocab_part, vocab_part, 0)
    packed = jnp.concatenate(
        [table_rows, gain_first[None], gain_second[None], jnp.zeros((14, width), bf16)], axis=0
    )
    (gathered,) = exchange(0, [Item(packed, "ch")])
    joined = jnp.concatenate([gathered[i] for i in range(n_ch)], axis=1)
    whole_gain_first, whole_gain_second = joined[vocab_part], joined[vocab_part + 1]
    table_normed, table_scale = normalise(joined[:vocab_part], whole_gain_first)
    table_projected = jnp.dot(table_normed, flat_first, preferred_element_type=f32).astype(bf16)
    projected_parts, normed_parts = exchange(
        1, [Item(table_projected, "seq"), Item(table_normed, "seq", window=1)]
    )
    table = jnp.concatenate([projected_parts.reshape(vocab, wide), embedding], axis=1)

    onehot = (ids[:, None] == jnp.arange(vocab, dtype=jnp.int32)[None, :]).astype(bf16)
    looked_up = jnp.dot(onehot, table, preferred_element_type=f32).astype(bf16)
    ahead = HALO - SUB
    featured_first = taps_ahead(looked_up[:, :wide], taps_first, SUB, looked_up.shape[0] - SUB)
    gated_first = (
        (featured_first[:, width : 2 * width] * featured_first[:, 2 * width :]).astype(bf16).astype(f32)
    )
    medium_float = medium.astype(f32)
    tap_count = medium.shape[0]
    out_rows = rows + 2 * LEAD
    begin = ahead - LEAD - (tap_count - 1)
    filtered_first = lag_sum(gated_first[begin : begin + out_rows + tap_count], medium_float)
    near = slice(ahead - LEAD, ahead - LEAD + out_rows)
    embedded = looked_up[HALO - LEAD : HALO - LEAD + out_rows, wide:].astype(f32)
    middle_near = (embedded + featured_first[near, :width] * filtered_first).astype(bf16)
    middle = middle_near[LEAD : LEAD + rows]

    whole_rows = lax.all_gather(middle_near, "ch", axis=1, tiled=True)
    normed_near, scale_near = normalise(whole_rows, whole_gain_second)
    normed_second, scale_second = normed_near[LEAD : LEAD + rows], scale_near[LEAD : LEAD + rows]
    projected_near = jnp.dot(normed_near, flat_second, preferred_element_type=f32).astype(bf16)
    featured_second = taps_ahead(projected_near, taps_second, LEAD, rows)
    pick = [featured_second[:, j * width : (j + 1) * width] for j in range(3)]
    gated_second = (pick[1] * pick[2]).astype(bf16).astype(f32)
    above_second = cotangent.astype(f32)
    grad_filtered = (above_second * pick[0]).astype(bf16).astype(f32)
    gated_lanes, grad_lanes = split_lanes(gated_second), split_lanes(grad_filtered)
    chunks, shard_states = mode_close(gated_lanes, grad_lanes, decay_rates)
    (all_states,) = exchange(2, [Item(shard_states, "seq")])
    other = jnp.arange(n_seq, dtype=jnp.int32)
    gaps = jnp.stack([seq_at - 1 - other, other - 1 - seq_at], axis=1)
    weights_of = jnp.where(
        (gaps >= 0)[:, :, None, None],
        jnp.exp(-decay_rates[None, None] * (jnp.maximum(gaps, 0) * rows).astype(f32)[:, :, None, None]),
        0.0,
    )
    entering = jnp.sum(weights_of * all_states, axis=0)
    filtered_lanes, gated_grad_lanes = mode_apply(
        gated_lanes, grad_lanes, decay_rates, residues, chunks, entering
    )
    filtered_second, grad_gated = join_lanes(filtered_lanes), join_lanes(gated_grad_lanes)
    output = (middle.astype(f32) + pick[0] * filtered_second).astype(bf16)

    grad_featured = jnp.concatenate(
        [above_second * filtered_second, grad_gated * pick[2], grad_gated * pick[1]], axis=1
    ).astype(bf16)
    following = shift_axis(grad_featured[:SUB], "seq", -1)
    grad_projected = taps_behind(
        jnp.concatenate([grad_featured, following], axis=0), taps_second, rows
    ).astype(bf16)
    row_part = jnp.sum(
        grad_projected.astype(f32) * projected_near[LEAD : LEAD + rows].astype(f32), axis=1
    )
    (row_total,) = exchange(3, [Item(small(row_part), "ch", reduce=True)])
    row_total = row_total.reshape(-1)[:rows]
    partial_sum = lax.dot_general(
        grad_projected, flat_second, (((1,), (1,)), ((), ())), preferred_element_type=f32
    ).astype(bf16)
    grad_normed = lax.psum_scatter(partial_sum, "ch", scatter_dimension=1, tiled=True).astype(f32)
    weight_grad_second = lax.psum_scatter(
        lax.dot_general(
            normed_second, grad_projected, (((0,), (0,)), ((), ())), preferred_element_type=f32
        ).astype(bf16),
        "seq",
        scatter_dimension=0,
        tiled=True,
    ).astype(f32)
    middle_float = middle.astype(f32)
    scale = scale_second[:, None]
    grad_middle = (
        above_second
        + scale * grad_normed * gain_second.astype(f32)
        - middle_float * (scale * scale) * row_total[:, None] / features
    ).astype(bf16)
    gain_part_second = jnp.sum(grad_normed * middle_float * scale, axis=0)

    grad_near = jnp.concatenate([grad_middle, shift_axis(grad_middle[:HALO], "seq", -1)], axis=0)
    from_here = slice(ahead, ahead + rows + HALO)
    grad_filtered = (
        (grad_near.astype(f32) * featured_first[from_here, :width]).astype(bf16).astype(f32)
    )
    grad_gated = lag_sum(grad_filtered, medium_float[::-1])[: rows + SUB]
    here = slice(ahead, ahead + rows + SUB)
    grad_featured = jnp.concatenate(
        [
            grad_near[: rows + SUB].astype(f32) * filtered_first[LEAD:],
            grad_gated * featured_first[here, 2 * width :],
            grad_gated * featured_first[here, width : 2 * width],
        ],
        axis=1,
    ).astype(bf16)
    grad_projected = taps_behind(grad_featured, taps_first, rows).astype(bf16)
    by_token = lax.dot_general(
        onehot[HALO : HALO + rows],
        jnp.concatenate([grad_projected, grad_middle], axis=1),
        (((0,), (0,)), ((), ())),
        preferred_element_type=f32,
    ).astype(bf16)
    (token_sums,) = exchange(4, [Item(by_token, "seq", window=0, reduce=True)])
    token_grad = token_sums[:, :wide].astype(bf16)
    token_above = token_sums[:, wide:]
    token_part = jnp.sum(token_grad.astype(f32) * table_projected.astype(f32), axis=1)
    token_partial = lax.dot_general(
        token_grad, flat_first, (((1,), (1,)), ((), ())), preferred_element_type=f32
    ).astype(bf16)
    spread = jnp.broadcast_to(token_part[:, None], (vocab_part, LANES))
    token_normed, token_total, token_grads = exchange(
        5,
        [
            Item(token_partial, "ch", window=1, reduce=True),
            Item(spread, "ch", reduce=True),
            Item(token_grad, "seq"),
        ],
    )
    table_float = table_rows.astype(f32)
    scale = table_scale[:, None]
    grad_table = (
        token_above
        + scale * token_normed * gain_first.astype(f32)
        - table_float * (scale * scale) * token_total[:, :1] / features
    )
    gain_part_first = jnp.sum(token_normed * table_float * scale, axis=0)
    gain_parts = jnp.concatenate(
        [gain_part_first[None], gain_part_second[None], jnp.zeros((6, width), f32)], axis=0
    )
    table_parts, gain_total = exchange(
        6, [Item(grad_table.astype(bf16), "seq"), Item(gain_parts, "seq", reduce=True)]
    )
    weight_grad_first = lax.dot_general(
        normed_parts.reshape(vocab, features // n_seq),
        token_grads.reshape(vocab, wide),
        (((0,), (0,)), ((), ())),
        preferred_element_type=f32,
    )
    return (
        output,
        table_parts.reshape(vocab, width).astype(f32),
        gain_total[0],
        gain_total[1],
        weight_grad_first.reshape(-1, 3, width),
        weight_grad_second.reshape(-1, 3, width),
    )


def solution(mesh):
    placed = (
        P("seq"),
        P(None, "ch"),
        P("ch"),
        P("ch"),
        P(None, None, "ch"),
        P(None, None, "ch"),
        P(None, None, "ch"),
        P(None, None, "ch"),
        P(None, "ch"),
        P(None, "ch"),
        P(None, "ch"),
        P("seq", "ch"),
    )
    return jax.shard_map(
        per_device,
        mesh=mesh,
        in_specs=placed,
        out_specs=(
            P("seq", "ch"),
            P(None, "ch"),
            P("ch"),
            P("ch"),
            P("seq", None, "ch"),
            P("seq", None, "ch"),
        ),
        check_vma=False,
    )
```

```python
import functools

import jax
import jax.numpy as jnp
from jax import lax
from jax.experimental import pallas as pl
from jax.experimental.pallas import tpu as pltpu
from jax.sharding import PartitionSpec as P

epsilon = 1e-06
MESH = pl.DeviceIdType.MESH
f32 = jnp.float32
bf16 = jnp.bfloat16
LANES = 128
SUB = 8
HALO = 144
LEAD = 8


class Item:
    def __init__(self, array, axis, window=None, reduce=False):
        self.array, self.axis, self.window, self.reduce = array, axis, window, reduce

    def block(self):
        shape = list(self.array.shape)
        if self.window is not None:
            shape[self.window] //= lax.axis_size(self.axis)
        return tuple(shape)


def exchange(cid, items):
    count = len(items)
    sizes = [lax.axis_size(it.axis) for it in items]
    blocks = [it.block() for it in items]
    axes = []
    for it in items:
        if it.axis not in axes:
            axes.append(it.axis)
    most = max(sizes)
    reduced = [k for k in range(count) if items[k].reduce]

    def body(*refs):
        srcs, outs = refs[:count], refs[count : 2 * count]
        bufs = list(outs)
        rest = refs[2 * count :]
        for slot, k in enumerate(reduced):
            bufs[k] = rest[slot]
        send_sem, recv_sem, own_sem = rest[len(reduced) :]

        def part(k, peer):
            if items[k].window is None:
                return srcs[k]
            width = blocks[k][items[k].window]
            start = pl.multiple_of(peer * width, width)
            index = [slice(None)] * len(blocks[k])
            index[items[k].window] = pl.ds(start, width)
            return srcs[k].at[tuple(index)]

        barrier = pltpu.get_barrier_semaphore()
        total = 0
        for axis in axes:
            n = lax.axis_size(axis)
            total += n - 1
            me = lax.axis_index(axis)

            def greet(step, carry, axis=axis, n=n, me=me):
                peer = lax.rem(me + step, n)
                pl.semaphore_signal(barrier, inc=1, device_id={axis: peer}, device_id_type=MESH)
                return carry

            lax.fori_loop(1, n, greet, 0)
        pl.semaphore_wait(barrier, total)

        def copy(k, peer, slot):
            me = lax.axis_index(items[k].axis)
            return pltpu.make_async_remote_copy(
                src_ref=part(k, peer),
                dst_ref=bufs[k].at[me],
                send_sem=send_sem.at[k, slot],
                recv_sem=recv_sem.at[k, me],
                device_id={items[k].axis: peer},
                device_id_type=MESH,
            )

        for k in range(count):
            n = sizes[k]
            me = lax.axis_index(items[k].axis)

            def push(step, carry, k=k, n=n, me=me):
                copy(k, lax.rem(me + step, n), step).start()
                return carry

            lax.fori_loop(1, n, push, 0)
        for k in range(count):
            me = lax.axis_index(items[k].axis)
            pltpu.make_async_copy(part(k, me), bufs[k].at[me], own_sem.at[k]).start()
        for k in range(count):
            n = sizes[k]
            me = lax.axis_index(items[k].axis)
            pltpu.make_async_copy(part(k, me), bufs[k].at[me], own_sem.at[k]).wait()

            def finish(step, carry, k=k, n=n, me=me):
                peer = lax.rem(me + step, n)
                copy(k, peer, step).wait_send()
                pltpu.make_async_remote_copy(
                    src_ref=part(k, peer),
                    dst_ref=bufs[k].at[peer],
                    send_sem=send_sem.at[k, step],
                    recv_sem=recv_sem.at[k, peer],
                    device_id={items[k].axis: peer},
                    device_id_type=MESH,
                ).wait_recv()
                return carry

            lax.fori_loop(1, n, finish, 0)
            if items[k].reduce:
                running = bufs[k][0].astype(f32)
                for j in range(1, n):
                    running = running + bufs[k][j].astype(f32)
                outs[k][...] = running

    shapes = []
    scratch = []
    for k in range(count):
        full = (sizes[k],) + blocks[k]
        if items[k].reduce:
            shapes.append(jax.ShapeDtypeStruct(blocks[k], f32))
            scratch.append(pltpu.VMEM(full, items[k].array.dtype))
        else:
            shapes.append(jax.ShapeDtypeStruct(full, items[k].array.dtype))
    scratch += [
        pltpu.SemaphoreType.DMA((count, most)),
        pltpu.SemaphoreType.DMA((count, most)),
        pltpu.SemaphoreType.DMA((count,)),
    ]
    vmem = pl.BlockSpec(memory_space=pltpu.VMEM)
    return pl.pallas_call(
        body,
        out_shape=shapes,
        in_specs=[vmem] * count,
        out_specs=[vmem] * count,
        scratch_shapes=scratch,
        compiler_params=pltpu.CompilerParams(collective_id=cid, has_side_effects=True),
        name=f"exchange_{cid}",
    )(*[it.array for it in items])


def place(x, z, core):
    return x * 8 + z * 2 + core


def spot():
    at = lax.axis_index("ch")
    return at // 8, lax.rem(at // 2, 4), lax.rem(at, 2)


def ring_gather(cid, block):
    rows, width = block.shape
    n = lax.axis_size("ch")
    cut = (rows // 2 + 15) // 16 * 16
    halves = ((0, cut), (cut, rows - cut))

    def body(src, out, send_sem, recv_sem, own_sem):
        x, z, core = spot()
        me = place(x, z, core)
        z_up, z_down, z_far = lax.rem(z + 1, 4), lax.rem(z + 3, 4), lax.rem(z + 2, 4)
        up, down, far = place(x, z_up, core), place(x, z_down, core), place(x, z_far, core)
        over, twin = place(1 - x, z, core), place(x, z, 1 - core)
        over_up, over_down = place(1 - x, z_up, core), place(1 - x, z_down, core)
        over_far = place(1 - x, z_far, core)

        barrier = pltpu.get_barrier_semaphore()
        for peer in (up, down, over, twin):
            pl.semaphore_signal(barrier, inc=1, device_id={"ch": peer}, device_id_type=MESH)
        pl.semaphore_wait(barrier, 4)

        def window(c, h):
            first, size = halves[h]
            return out.at[pl.ds(first, size), pl.ds(pl.multiple_of(c * width, width), width)]

        sends = []

        def send(c, h, to, ref=None):
            copy = pltpu.make_async_remote_copy(
                src_ref=window(c, h) if ref is None else ref,
                dst_ref=window(c, h),
                send_sem=send_sem.at[len(sends)],
                recv_sem=recv_sem.at[c, h],
                device_id={"ch": to},
                device_id_type=MESH,
            )
            copy.start()
            sends.append(copy)

        def arrive(c, h):
            pltpu.make_async_remote_copy(
                src_ref=window(c, h),
                dst_ref=window(c, h),
                send_sem=send_sem.at[0],
                recv_sem=recv_sem.at[c, h],
                device_id={"ch": twin},
                device_id_type=MESH,
            ).wait_recv()

        mine = [src.at[pl.ds(first, size), :] for first, size in halves]
        for h, to in ((0, up), (1, down), (0, over), (1, over), (1, up), (0, down), (0, twin), (1, twin)):
            send(me, h, to, mine[h])
        own = pltpu.make_async_copy(
            src, out.at[:, pl.ds(pl.multiple_of(me * width, width), width)], own_sem
        )
        own.start()
        arrive(down, 0)
        send(down, 0, up)
        arrive(up, 1)
        send(up, 1, down)
        send(down, 0, twin)
        send(up, 1, twin)
        for h in (0, 1):
            arrive(over, h)
            send(over, h, up)
            send(over, h, down)
            send(over, h, twin)
        arrive(down, 1)
        send(down, 1, twin)
        arrive(up, 0)
        send(up, 0, twin)
        arrive(over_down, 0)
        send(over_down, 0, up)
        arrive(over_up, 1)
        send(over_up, 1, down)
        for c, h in ((far, 0), (far, 1)):
            arrive(c, h)
            send(c, h, twin)
        send(over_down, 0, twin)
        send(over_up, 1, twin)
        for c, h in ((over_down, 1), (over_up, 0), (over_far, 0), (over_far, 1)):
            arrive(c, h)
            send(c, h, twin)
        for px in (0, 1):
            for pz in range(4):
                for h in (0, 1):
                    arrive(place(px, pz, 1 - core), h)
        own.wait()
        for copy in sends:
            copy.wait_send()

    vmem = pl.BlockSpec(memory_space=pltpu.VMEM)
    return pl.pallas_call(
        body,
        out_shape=jax.ShapeDtypeStruct((rows, n * width), block.dtype),
        in_specs=[vmem],
        out_specs=vmem,
        scratch_shapes=[
            pltpu.SemaphoreType.DMA((32,)),
            pltpu.SemaphoreType.DMA((n, 2)),
            pltpu.SemaphoreType.DMA,
        ],
        compiler_params=pltpu.CompilerParams(collective_id=cid, has_side_effects=True),
        name=f"ring_gather_{cid}",
    )(block)


def ring_scatter(cid, partial, row_part):
    rows, columns = partial.shape
    n = lax.axis_size("ch")
    width = columns // n
    half = rows // 2
    step_rows = 32

    def body(part, row_in, out, row_out, mate, acc, fwd, blk, cross, mine, row_buf, sems, row_send, row_recv):
        x, z, core = spot()
        me = place(x, z, core)
        z_up, z_down, z_far = lax.rem(z + 1, 4), lax.rem(z + 3, 4), lax.rem(z + 2, 4)
        up, down = place(x, z_up, core), place(x, z_down, core)
        over, twin = place(1 - x, z, core), place(x, z, 1 - core)
        barrier = pltpu.get_barrier_semaphore()

        def greet(step, carry):
            peer = lax.rem(me + step, n)
            pl.semaphore_signal(barrier, inc=1, device_id={"ch": peer}, device_id_type=MESH)
            return carry

        lax.fori_loop(1, n, greet, 0)
        pl.semaphore_wait(barrier, n - 1)

        def columns_of(px, pz, pk):
            return pl.ds(pl.multiple_of(place(px, pz, pk) * width, width), width)

        order = []
        for px in (1 - x, x):
            for pz in (z_far, z_up, z_down, z):
                order.append((px, pz))

        def remote(src, dst, k, to):
            return pltpu.make_async_remote_copy(
                src_ref=src,
                dst_ref=dst,
                send_sem=sems.at[0, k],
                recv_sem=sems.at[1, k],
                device_id={"ch": to},
                device_id_type=MESH,
            )

        firsts = []
        for i, (px, pz) in enumerate(order):
            copy = remote(part.at[:, columns_of(px, pz, 1 - core)], mate.at[i], i, twin)
            copy.start()
            firsts.append(copy)

        def row_copy(peer, slot):
            return pltpu.make_async_remote_copy(
                src_ref=row_in,
                dst_ref=row_buf.at[me],
                send_sem=row_send.at[slot],
                recv_sem=row_recv.at[me],
                device_id={"ch": peer},
                device_id_type=MESH,
            )

        def push_row(step, carry):
            row_copy(lax.rem(me + step, n), step).start()
            return carry

        lax.fori_loop(1, n, push_row, 0)

        def add(target, sources, first, size):
            def chunk(i, carry):
                at = pl.ds(pl.multiple_of(first + i * step_rows, step_rows), step_rows)
                total = None
                for ref, base in sources:
                    index = pl.ds(pl.multiple_of(first - base + i * step_rows, step_rows), step_rows)
                    term = ref[index, :].astype(f32)
                    total = term if total is None else total + term
                target[at, :] = total.astype(target.dtype)
                return carry

            lax.fori_loop(0, size // step_rows, chunk, 0)

        def meet(i):
            px, pz = order[i]
            firsts[i].wait_recv()
            add(acc.at[i], ((part.at[:, columns_of(px, pz, core)], 0), (mate.at[i], 0)), 0, rows)

        pending = []
        slots = 8

        def begin(p):
            base = 4 * p
            meet(base)
            k = slots + 4 * p
            a = remote(acc.at[base, pl.ds(0, half), :], fwd.at[p, 0], k, up)
            b = remote(acc.at[base, pl.ds(half, half), :], fwd.at[p, 1], k + 1, down)
            a.start()
            b.start()
            meet(base + 1)
            meet(base + 2)
            meet(base + 3)
            return a, b

        def middle(p, pair):
            base, k = 4 * p, slots + 4 * p
            a, b = pair
            a.wait_recv()
            add(acc.at[base + 1], ((acc.at[base + 1], 0), (fwd.at[p, 0], 0)), 0, half)
            c = remote(acc.at[base + 1], blk.at[p, 0], k + 2, up)
            c.start()
            b.wait_recv()
            add(acc.at[base + 2], ((acc.at[base + 2], 0), (fwd.at[p, 1], half)), half, half)
            d = remote(acc.at[base + 2], blk.at[p, 1], k + 3, down)
            d.start()
            return c, d

        pair = begin(0)
        blocks = middle(0, pair)
        pair_own = begin(1)
        blocks_own = middle(1, pair_own)
        for copy in blocks:
            copy.wait_recv()
        add(mine, ((acc.at[3], 0), (blk.at[0, 0], 0), (blk.at[0, 1], 0)), 0, rows)
        crossing = remote(mine, cross, slots + 8, over)
        crossing.start()
        for copy in blocks_own:
            copy.wait_recv()
        crossing.wait_recv()
        add(out, ((acc.at[7], 0), (blk.at[1, 0], 0), (blk.at[1, 1], 0), (cross, 0)), 0, rows)
        for copy in [*firsts, *pair, *blocks, *pair_own, *blocks_own, crossing]:
            copy.wait_send()

        def gather_row(step, carry):
            peer = lax.rem(me + step, n)
            row_copy(peer, step).wait_send()
            pltpu.make_async_remote_copy(
                src_ref=row_in,
                dst_ref=row_buf.at[peer],
                send_sem=row_send.at[step],
                recv_sem=row_recv.at[peer],
                device_id={"ch": peer},
                device_id_type=MESH,
            ).wait_recv()
            return carry + row_buf[peer]

        row_out[...] = lax.fori_loop(1, n, gather_row, row_in[...])

    vmem = pl.BlockSpec(memory_space=pltpu.VMEM)
    return pl.pallas_call(
        body,
        out_shape=[
            jax.ShapeDtypeStruct((rows, width), f32),
            jax.ShapeDtypeStruct(row_part.shape, f32),
        ],
        in_specs=[vmem] * 2,
        out_specs=[vmem] * 2,
        scratch_shapes=[
            pltpu.VMEM((8, rows, width), bf16),
            pltpu.VMEM((8, rows, width), bf16),
            pltpu.VMEM((2, 2, half, width), bf16),
            pltpu.VMEM((2, 2, rows, width), bf16),
            pltpu.VMEM((rows, width), bf16),
            pltpu.VMEM((rows, width), bf16),
            pltpu.VMEM((n,) + row_part.shape, f32),
            pltpu.SemaphoreType.DMA((2, 17)),
            pltpu.SemaphoreType.DMA((n,)),
            pltpu.SemaphoreType.DMA((n,)),
        ],
        compiler_params=pltpu.CompilerParams(collective_id=cid, has_side_effects=True),
        name=f"ring_scatter_{cid}",
    )(partial, row_part)


def lag_sum(x, taps):
    tap_count, width = taps.shape
    rows = x.shape[0] - tap_count
    length = rows // SUB
    span = length + tap_count - 1
    group = 11
    tap_group = 8

    def body(x_ref, taps_ref, y_ref, spread, wide):
        for lane in range(width // LANES):
            lanes = slice(lane * LANES, (lane + 1) * LANES)

            def arrange(q, carry):
                spread[q] = x_ref[lane, pl.ds(q, SUB, stride=length), :]
                return carry

            lax.fori_loop(0, span, arrange, 0)

            def widen(k, carry):
                eight = taps_ref[pl.ds(pl.multiple_of(k * SUB, SUB), SUB), lanes]
                for i in range(SUB):
                    wide[k * SUB + i] = jnp.broadcast_to(eight[i : i + 1], (SUB, LANES))
                return carry

            lax.fori_loop(0, tap_count // SUB, widen, 0)

            def block(b, carry):
                first = b * group

                def add(kb, sums):
                    base = first + (tap_count - tap_group) - kb * tap_group
                    window = [spread[base + w] for w in range(group + tap_group - 1)]
                    out = list(sums)
                    for kk in range(tap_group):
                        tap = wide[kb * tap_group + kk]
                        for r in range(group):
                            out[r] = out[r] + tap * window[r + tap_group - 1 - kk]
                    return tuple(out)

                zero = tuple(jnp.zeros((SUB, LANES), f32) for _ in range(group))
                sums = lax.fori_loop(0, tap_count // tap_group, add, zero)
                for r in range(group):
                    y_ref[lane, pl.ds(first + r, SUB, stride=length), :] = sums[r]
                return carry

            lax.fori_loop(0, length // group, block, 0)

    vmem = pl.BlockSpec(memory_space=pltpu.VMEM)
    lanes_first = jnp.stack([x[:, i : i + LANES] for i in range(0, width, LANES)], axis=0)
    y = pl.pallas_call(
        body,
        out_shape=jax.ShapeDtypeStruct((width // LANES, rows, LANES), f32),
        in_specs=[vmem, vmem],
        out_specs=vmem,
        scratch_shapes=[
            pltpu.VMEM((span, SUB, LANES), f32),
            pltpu.VMEM((tap_count, SUB, LANES), f32),
        ],
        name="lag_sum",
    )(lanes_first, taps)
    return jnp.concatenate([y[i] for i in range(width // LANES)], axis=1)


def split_lanes(x):
    return jnp.stack([x[:, i : i + LANES] for i in range(0, x.shape[1], LANES)], axis=0)


def join_lanes(x):
    return jnp.concatenate([x[i] for i in range(x.shape[0])], axis=1)


def mode_close(ahead, behind, rates):
    groups, rows, _ = ahead.shape
    modes, width = rates.shape
    length = rows // SUB
    unroll = 4

    def body(a_ref, b_ref, rate_ref, chunk_ref, shard_ref):
        order = lax.broadcasted_iota(jnp.int32, (SUB, LANES), 0).astype(f32)
        for way, src in enumerate((a_ref, b_ref)):
            for lane in range(groups):
                lanes = slice(lane * LANES, (lane + 1) * LANES)
                rate = [jnp.broadcast_to(rate_ref[m : m + 1, lanes], (SUB, LANES)) for m in range(modes)]
                decay = [jnp.exp(-r) for r in rate]

                def step(i, states):
                    states = list(states)
                    for u in range(unroll):
                        r = i * unroll + u
                        if way == 1:
                            r = length - 1 - r
                        x = src[lane, pl.ds(r, SUB, stride=length), :]
                        states = [decay[m] * states[m] + x for m in range(modes)]
                    return tuple(states)

                zero = tuple(jnp.zeros((SUB, LANES), f32) for _ in range(modes))
                states = lax.fori_loop(0, length // unroll, step, zero)
                after = (SUB - 1) - order if way == 0 else order
                for m in range(modes):
                    chunk_ref[way, m, :, lanes] = states[m]
                    weighted = states[m] * jnp.exp(-(rate[m] * (after * float(length))))
                    shard_ref[way, m : m + 1, lanes] = jnp.sum(weighted, axis=0, keepdims=True)

    vmem = pl.BlockSpec(memory_space=pltpu.VMEM)
    return pl.pallas_call(
        body,
        out_shape=[
            jax.ShapeDtypeStruct((2, modes, SUB, width), f32),
            jax.ShapeDtypeStruct((2, modes, width), f32),
        ],
        in_specs=[vmem] * 3,
        out_specs=[vmem] * 2,
        name="mode_close",
    )(ahead, behind, rates)


def mode_apply(ahead, behind, rates, residues, chunks, entering):
    groups, rows, _ = ahead.shape
    modes, width = rates.shape
    length = rows // SUB
    unroll = 2

    def body(a_ref, b_ref, rate_ref, res_ref, chunk_ref, enter_ref, ya_ref, yb_ref):
        order = lax.broadcasted_iota(jnp.int32, (SUB, LANES), 0)
        for way, (src, dst) in enumerate(((a_ref, ya_ref), (b_ref, yb_ref))):
            place = order if way == 0 else (SUB - 1) - order
            for lane in range(groups):
                lanes = slice(lane * LANES, (lane + 1) * LANES)
                decay = []
                residue = []
                start = []
                for m in range(modes):
                    rate = jnp.broadcast_to(rate_ref[m : m + 1, lanes], (SUB, LANES))
                    decay.append(jnp.exp(-rate))
                    residue.append(jnp.broadcast_to(res_ref[m : m + 1, lanes], (SUB, LANES)))
                    first = jnp.broadcast_to(enter_ref[way, m : m + 1, lanes], (SUB, LANES))

                    def back(v, by):
                        moved = pltpu.roll(v, by if way == 0 else SUB - by, 0)
                        return moved

                    state = jnp.where(place == 0, first, back(chunk_ref[way, m, :, lanes], 1))
                    for by in (1, 2, 4):
                        factor = jnp.exp(-(rate * float(by * length)))
                        state = state + jnp.where(place >= by, factor * back(state, by), 0.0)
                    start.append(state)

                def step(i, states):
                    states = list(states)
                    for u in range(unroll):
                        r = i * unroll + u
                        if way == 1:
                            r = length - 1 - r
                        x = src[lane, pl.ds(r, SUB, stride=length), :]
                        states = [decay[m] * states[m] + x for m in range(modes)]
                        terms = [residue[m] * states[m] for m in range(modes)]
                        while len(terms) > 1:
                            terms = [a + b for a, b in zip(terms[::2], terms[1::2])]
                        dst[lane, pl.ds(r, SUB, stride=length), :] = terms[0]
                    return tuple(states)

                lax.fori_loop(0, length // unroll, step, tuple(start))

    vmem = pl.BlockSpec(memory_space=pltpu.VMEM)
    return pl.pallas_call(
        body,
        out_shape=[jax.ShapeDtypeStruct(ahead.shape, f32)] * 2,
        in_specs=[vmem] * 6,
        out_specs=[vmem] * 2,
        name="mode_apply",
    )(ahead, behind, rates, residues, chunks, entering)


def shift_axis(shard, axis, by):
    n = lax.axis_size(axis)
    pairs = [(i, i + by) for i in range(n) if 0 <= i + by < n]
    return lax.ppermute(shard, axis, pairs)


def taps_ahead(projected, short_filter, first, rows):
    tap_count = short_filter.shape[0]
    running = None
    for i in range(tap_count):
        term = short_filter[i] * projected[first - i : first - i + rows].astype(f32)
        running = term if running is None else running + term
    return running


def taps_behind(gradient, short_filter, rows):
    running = None
    for i in range(short_filter.shape[0]):
        term = short_filter[i] * gradient[i : i + rows].astype(f32)
        running = term if running is None else running + term
    return running


def normalise(whole, gain):
    as_float = whole.astype(f32)
    scale = lax.rsqrt(jnp.mean(as_float * as_float, axis=1) + epsilon)
    return (as_float * scale[:, None] * gain[None, :].astype(f32)).astype(bf16), scale


def small(vector, lanes=LANES):
    rows = vector.reshape(-1, lanes)
    pad = -rows.shape[0] % SUB
    return jnp.pad(rows, ((0, pad), (0, 0)))


def per_device(
    token_ids,
    embedding,
    gain_first,
    gain_second,
    weights_first,
    weights_second,
    short_first,
    short_second,
    medium,
    residues,
    decay_rates,
    cotangent,
):
    n_seq, n_ch = lax.axis_size("seq"), lax.axis_size("ch")
    seq_at = lax.axis_index("seq")
    rows = token_ids.shape[0]
    vocab, width = embedding.shape
    features = weights_first.shape[0]
    wide = 3 * width
    vocab_part = vocab // n_seq
    flat_first = weights_first.reshape(features, wide)
    flat_second = weights_second.reshape(features, wide)
    taps_first = short_first.reshape(-1, wide)
    taps_second = short_second.reshape(-1, wide)

    shifted = token_ids + 1
    ids = jnp.concatenate(
        [
            shift_axis(shifted[rows - HALO :], "seq", 1),
            shifted,
            shift_axis(shifted[:HALO], "seq", -1),
        ]
    ) - 1

    packed = jnp.concatenate(
        [embedding, gain_first[None], gain_second[None], jnp.zeros((14, width), bf16)], axis=0
    )
    joined = ring_gather(0, packed)
    whole_gain_first, whole_gain_second = joined[vocab], joined[vocab + 1]
    table_normed, table_scale = normalise(joined[:vocab], whole_gain_first)
    table_projected = jnp.dot(table_normed, flat_first, preferred_element_type=f32).astype(bf16)
    table = jnp.concatenate([table_projected, embedding], axis=1)

    onehot = (ids[:, None] == jnp.arange(vocab, dtype=jnp.int32)[None, :]).astype(bf16)
    looked_up = jnp.dot(onehot, table, preferred_element_type=f32).astype(bf16)
    ahead = HALO - SUB
    featured_first = taps_ahead(looked_up[:, :wide], taps_first, SUB, looked_up.shape[0] - SUB)
    gated_first = (
        (featured_first[:, width : 2 * width] * featured_first[:, 2 * width :]).astype(bf16).astype(f32)
    )
    medium_float = medium.astype(f32)
    tap_count = medium.shape[0]
    out_rows = rows + 2 * LEAD
    begin = ahead - LEAD - (tap_count - 1)
    filtered_first = lag_sum(gated_first[begin : begin + out_rows + tap_count], medium_float)
    near = slice(ahead - LEAD, ahead - LEAD + out_rows)
    embedded = looked_up[HALO - LEAD : HALO - LEAD + out_rows, wide:].astype(f32)
    middle_near = (embedded + featured_first[near, :width] * filtered_first).astype(bf16)
    middle = middle_near[LEAD : LEAD + rows]

    whole_rows = ring_gather(1, middle_near)
    normed_near, scale_near = normalise(whole_rows, whole_gain_second)
    normed_second, scale_second = normed_near[LEAD : LEAD + rows], scale_near[LEAD : LEAD + rows]
    projected_near = jnp.dot(normed_near, flat_second, preferred_element_type=f32).astype(bf16)
    featured_second = taps_ahead(projected_near, taps_second, LEAD, rows)
    pick = [featured_second[:, j * width : (j + 1) * width] for j in range(3)]
    gated_second = (pick[1] * pick[2]).astype(bf16).astype(f32)
    above_second = cotangent.astype(f32)
    grad_filtered = (above_second * pick[0]).astype(bf16).astype(f32)
    gated_lanes, grad_lanes = split_lanes(gated_second), split_lanes(grad_filtered)
    chunks, shard_states = mode_close(gated_lanes, grad_lanes, decay_rates)
    (all_states,) = exchange(2, [Item(shard_states, "seq")])
    other = jnp.arange(n_seq, dtype=jnp.int32)
    gaps = jnp.stack([seq_at - 1 - other, other - 1 - seq_at], axis=1)
    weights_of = jnp.where(
        (gaps >= 0)[:, :, None, None],
        jnp.exp(-decay_rates[None, None] * (jnp.maximum(gaps, 0) * rows).astype(f32)[:, :, None, None]),
        0.0,
    )
    entering = jnp.sum(weights_of * all_states, axis=0)
    filtered_lanes, gated_grad_lanes = mode_apply(
        gated_lanes, grad_lanes, decay_rates, residues, chunks, entering
    )
    filtered_second, grad_gated = join_lanes(filtered_lanes), join_lanes(gated_grad_lanes)
    output = (middle.astype(f32) + pick[0] * filtered_second).astype(bf16)

    grad_featured = jnp.concatenate(
        [above_second * filtered_second, grad_gated * pick[2], grad_gated * pick[1]], axis=1
    ).astype(bf16)
    following = shift_axis(grad_featured[:SUB], "seq", -1)
    grad_projected = taps_behind(
        jnp.concatenate([grad_featured, following], axis=0), taps_second, rows
    ).astype(bf16)
    row_part = jnp.sum(
        grad_projected.astype(f32) * projected_near[LEAD : LEAD + rows].astype(f32), axis=1
    )
    partial_sum = lax.dot_general(
        grad_projected, flat_second, (((1,), (1,)), ((), ())), preferred_element_type=f32
    ).astype(bf16)
    grad_normed, row_total = ring_scatter(3, partial_sum, small(row_part))
    row_total = row_total.reshape(-1)[:rows]
    weight_grad_second = lax.psum_scatter(
        lax.dot_general(
            normed_second, grad_projected, (((0,), (0,)), ((), ())), preferred_element_type=f32
        ).astype(bf16),
        "seq",
        scatter_dimension=0,
        tiled=True,
    ).astype(f32)
    middle_float = middle.astype(f32)
    scale = scale_second[:, None]
    grad_middle = (
        above_second
        + scale * grad_normed * gain_second.astype(f32)
        - middle_float * (scale * scale) * row_total[:, None] / features
    ).astype(bf16)
    gain_part_second = jnp.sum(grad_normed * middle_float * scale, axis=0)

    grad_near = jnp.concatenate([grad_middle, shift_axis(grad_middle[:HALO], "seq", -1)], axis=0)
    from_here = slice(ahead, ahead + rows + HALO)
    grad_filtered = (
        (grad_near.astype(f32) * featured_first[from_here, :width]).astype(bf16).astype(f32)
    )
    grad_gated = lag_sum(grad_filtered, medium_float[::-1])[: rows + SUB]
    here = slice(ahead, ahead + rows + SUB)
    grad_featured = jnp.concatenate(
        [
            grad_near[: rows + SUB].astype(f32) * filtered_first[LEAD:],
            grad_gated * featured_first[here, 2 * width :],
            grad_gated * featured_first[here, width : 2 * width],
        ],
        axis=1,
    ).astype(bf16)
    grad_projected = taps_behind(grad_featured, taps_first, rows).astype(bf16)
    by_token = lax.dot_general(
        onehot[HALO : HALO + rows],
        jnp.concatenate([grad_projected, grad_middle], axis=1),
        (((0,), (0,)), ((), ())),
        preferred_element_type=f32,
    ).astype(bf16)
    (token_sums,) = exchange(4, [Item(by_token, "seq", window=0, reduce=True)])
    token_grad = token_sums[:, :wide].astype(bf16)
    token_above = token_sums[:, wide:]
    own_part = lambda array: lax.dynamic_slice_in_dim(array, seq_at * vocab_part, vocab_part, 0)
    token_part = jnp.sum(token_grad.astype(f32) * own_part(table_projected).astype(f32), axis=1)
    token_partial = lax.dot_general(
        token_grad, flat_first, (((1,), (1,)), ((), ())), preferred_element_type=f32
    ).astype(bf16)
    spread = jnp.broadcast_to(token_part[:, None], (vocab_part, LANES))
    token_normed, token_total, token_grads = exchange(
        5,
        [
            Item(token_partial, "ch", window=1, reduce=True),
            Item(spread, "ch", reduce=True),
            Item(token_grad, "seq"),
        ],
    )
    table_float = own_part(embedding).astype(f32)
    scale = own_part(table_scale)[:, None]
    grad_table = (
        token_above
        + scale * token_normed * gain_first.astype(f32)
        - table_float * (scale * scale) * token_total[:, :1] / features
    )
    gain_part_first = jnp.sum(token_normed * table_float * scale, axis=0)
    gain_parts = jnp.concatenate(
        [gain_part_first[None], gain_part_second[None], jnp.zeros((6, width), f32)], axis=0
    )
    table_parts, gain_total = exchange(
        6, [Item(grad_table.astype(bf16), "seq"), Item(gain_parts, "seq", reduce=True)]
    )
    weight_grad_first = lax.dot_general(
        lax.dynamic_slice_in_dim(table_normed, seq_at * (features // n_seq), features // n_seq, 1),
        token_grads.reshape(vocab, wide),
        (((0,), (0,)), ((), ())),
        preferred_element_type=f32,
    )
    return (
        output,
        table_parts.reshape(vocab, width).astype(f32),
        gain_total[0],
        gain_total[1],
        weight_grad_first.reshape(-1, 3, width),
        weight_grad_second.reshape(-1, 3, width),
    )


def solution(mesh):
    placed = (
        P("seq"),
        P(None, "ch"),
        P("ch"),
        P("ch"),
        P(None, None, "ch"),
        P(None, None, "ch"),
        P(None, None, "ch"),
        P(None, None, "ch"),
        P(None, "ch"),
        P(None, "ch"),
        P(None, "ch"),
        P("seq", "ch"),
    )
    return jax.shard_map(
        per_device,
        mesh=mesh,
        in_specs=placed,
        out_specs=(
            P("seq", "ch"),
            P(None, "ch"),
            P("ch"),
            P("ch"),
            P("seq", None, "ch"),
            P("seq", None, "ch"),
        ),
        check_vma=False,
    )
```

```python
import jax
import jax.numpy as jnp
from jax import lax
from jax.experimental import pallas as pl
from jax.experimental.pallas import tpu as pltpu
from jax.sharding import PartitionSpec as P


epsilon = 1e-06
MESH = pl.DeviceIdType.MESH
f32 = jnp.float32
bf16 = jnp.bfloat16
LANES = 128
SUB = 8
HALO = 144
LEAD = 8


class Item:
    def __init__(self, array, axis, window=None, reduce=False):
        self.array, self.axis, self.window, self.reduce = array, axis, window, reduce

    def block(self):
        shape = list(self.array.shape)
        if self.window == "onward":
            return tuple(shape[1:])
        if self.window is not None:
            shape[self.window] //= lax.axis_size(self.axis)
        return tuple(shape)


def exchange(cid, items):
    count = len(items)
    sizes = [lax.axis_size(it.axis) for it in items]
    blocks = [it.block() for it in items]
    axes = []
    for it in items:
        if it.axis not in axes:
            axes.append(it.axis)
    most = max(sizes)
    reduced = [k for k in range(count) if items[k].reduce]

    def body(*refs):
        srcs, outs = refs[:count], refs[count : 2 * count]
        bufs = list(outs)
        rest = refs[2 * count :]
        for slot, k in enumerate(reduced):
            bufs[k] = rest[slot]
        send_sem, recv_sem, own_sem = rest[len(reduced) :]

        def part(k, peer):
            if items[k].window is None:
                return srcs[k]
            if items[k].window == "onward":
                return srcs[k].at[jnp.where(peer > lax.axis_index(items[k].axis), 0, 1)]
            width = blocks[k][items[k].window]
            start = pl.multiple_of(peer * width, width)
            index = [slice(None)] * len(blocks[k])
            index[items[k].window] = pl.ds(start, width)
            return srcs[k].at[tuple(index)]

        barrier = pltpu.get_barrier_semaphore()
        total = 0
        for axis in axes:
            n = lax.axis_size(axis)
            total += n - 1
            me = lax.axis_index(axis)

            def greet(step, carry, axis=axis, n=n, me=me):
                peer = lax.rem(me + step, n)
                pl.semaphore_signal(barrier, inc=1, device_id={axis: peer}, device_id_type=MESH)
                return carry

            lax.fori_loop(1, n, greet, 0)
        pl.semaphore_wait(barrier, total)

        def copy(k, peer, slot):
            me = lax.axis_index(items[k].axis)
            return pltpu.make_async_remote_copy(
                src_ref=part(k, peer),
                dst_ref=bufs[k].at[me],
                send_sem=send_sem.at[k, slot],
                recv_sem=recv_sem.at[k, me],
                device_id={items[k].axis: peer},
                device_id_type=MESH,
            )

        for k in range(count):
            n = sizes[k]
            me = lax.axis_index(items[k].axis)

            def push(step, carry, k=k, n=n, me=me):
                copy(k, lax.rem(me + step, n), step).start()
                return carry

            lax.fori_loop(1, n, push, 0)
        for k in range(count):
            me = lax.axis_index(items[k].axis)
            pltpu.make_async_copy(part(k, me), bufs[k].at[me], own_sem.at[k]).start()
        for k in range(count):
            n = sizes[k]
            me = lax.axis_index(items[k].axis)
            pltpu.make_async_copy(part(k, me), bufs[k].at[me], own_sem.at[k]).wait()

            def finish(step, carry, k=k, n=n, me=me):
                peer = lax.rem(me + step, n)
                copy(k, peer, step).wait_send()
                pltpu.make_async_remote_copy(
                    src_ref=part(k, peer),
                    dst_ref=bufs[k].at[peer],
                    send_sem=send_sem.at[k, step],
                    recv_sem=recv_sem.at[k, peer],
                    device_id={items[k].axis: peer},
                    device_id_type=MESH,
                ).wait_recv()
                return carry

            lax.fori_loop(1, n, finish, 0)
            if items[k].reduce:
                running = bufs[k][0].astype(f32)
                for j in range(1, n):
                    running = running + bufs[k][j].astype(f32)
                outs[k][...] = running

    shapes = []
    scratch = []
    for k in range(count):
        full = (sizes[k],) + blocks[k]
        if items[k].reduce:
            shapes.append(jax.ShapeDtypeStruct(blocks[k], f32))
            scratch.append(pltpu.VMEM(full, items[k].array.dtype))
        else:
            shapes.append(jax.ShapeDtypeStruct(full, items[k].array.dtype))
    scratch += [
        pltpu.SemaphoreType.DMA((count, most)),
        pltpu.SemaphoreType.DMA((count, most)),
        pltpu.SemaphoreType.DMA((count,)),
    ]
    vmem = pl.BlockSpec(memory_space=pltpu.VMEM)
    return pl.pallas_call(
        body,
        out_shape=shapes,
        in_specs=[vmem] * count,
        out_specs=[vmem] * count,
        scratch_shapes=scratch,
        compiler_params=pltpu.CompilerParams(collective_id=cid, has_side_effects=True),
    )(*[it.array for it in items])


def place(x, z, core):
    return x * 8 + z * 2 + core


def spot():
    at = lax.axis_index("ch")
    return at // 8, lax.rem(at // 2, 4), lax.rem(at, 2)


def ring_gather(cid, block, tokens=None):
    rows, width = block.shape
    n = lax.axis_size("ch")
    cut = (rows // 2 + 15) // 16 * 16
    halves = ((0, cut), (cut, rows - cut))

    def body(*refs):
        if tokens is None:
            src, out, send_sem, recv_sem, own_sem = refs
        else:
            src, token_in, out, token_out, send_sem, recv_sem, own_sem, token_sem = refs
        x, z, core = spot()
        me = place(x, z, core)
        z_up, z_down, z_far = lax.rem(z + 1, 4), lax.rem(z + 3, 4), lax.rem(z + 2, 4)
        up, down, far = place(x, z_up, core), place(x, z_down, core), place(x, z_far, core)
        over, twin = place(1 - x, z, core), place(x, z, 1 - core)
        over_up, over_down = place(1 - x, z_up, core), place(1 - x, z_down, core)
        over_far = place(1 - x, z_far, core)

        barrier = pltpu.get_barrier_semaphore()
        for peer in (up, down, over, twin):
            pl.semaphore_signal(barrier, inc=1, device_id={"ch": peer}, device_id_type=MESH)
        token_copies = []
        if tokens is None:
            pl.semaphore_wait(barrier, 4)
        else:
            shards = lax.axis_size("seq")
            at = lax.axis_index("seq")
            for slot, peer in ((0, lax.rem(at + 1, shards)), (1, lax.rem(at + shards - 1, shards))):
                pl.semaphore_signal(barrier, inc=1, device_id={"seq": peer}, device_id_type=MESH)
                token_copies.append(
                    pltpu.make_async_remote_copy(
                        src_ref=token_in,
                        dst_ref=token_out.at[slot],
                        send_sem=token_sem.at[0, slot],
                        recv_sem=token_sem.at[1, slot],
                        device_id={"seq": peer},
                        device_id_type=MESH,
                    )
                )
            pl.semaphore_wait(barrier, 6)

        def window(c, h):
            first, size = halves[h]
            return out.at[pl.ds(first, size), pl.ds(pl.multiple_of(c * width, width), width)]

        sends = []

        def send(c, h, to, ref=None):
            copy = pltpu.make_async_remote_copy(
                src_ref=window(c, h) if ref is None else ref,
                dst_ref=window(c, h),
                send_sem=send_sem.at[len(sends)],
                recv_sem=recv_sem.at[c, h],
                device_id={"ch": to},
                device_id_type=MESH,
            )
            copy.start()
            sends.append(copy)

        def arrive(c, h):
            pltpu.make_async_remote_copy(
                src_ref=window(c, h),
                dst_ref=window(c, h),
                send_sem=send_sem.at[0],
                recv_sem=recv_sem.at[c, h],
                device_id={"ch": twin},
                device_id_type=MESH,
            ).wait_recv()

        mine = [src.at[pl.ds(first, size), :] for first, size in halves]
        for h, to in ((0, up), (1, down), (0, over), (1, over), (1, up), (0, down), (0, twin), (1, twin)):
            send(me, h, to, mine[h])
        own = pltpu.make_async_copy(
            src, out.at[:, pl.ds(pl.multiple_of(me * width, width), width)], own_sem
        )
        own.start()
        for copy in token_copies:
            copy.start()
        arrive(down, 0)
        send(down, 0, up)
        arrive(up, 1)
        send(up, 1, down)
        send(down, 0, twin)
        send(up, 1, twin)
        for h in (0, 1):
            arrive(over, h)
            send(over, h, up)
            send(over, h, down)
            send(over, h, twin)
        arrive(down, 1)
        send(down, 1, twin)
        arrive(up, 0)
        send(up, 0, twin)
        arrive(over_down, 0)
        send(over_down, 0, up)
        arrive(over_up, 1)
        send(over_up, 1, down)
        for c, h in ((far, 0), (far, 1)):
            arrive(c, h)
            send(c, h, twin)
        send(over_down, 0, twin)
        send(over_up, 1, twin)
        for c, h in ((over_down, 1), (over_up, 0), (over_far, 0), (over_far, 1)):
            arrive(c, h)
            send(c, h, twin)
        for px in (0, 1):
            for pz in range(4):
                for h in (0, 1):
                    arrive(place(px, pz, 1 - core), h)
        own.wait()
        for copy in sends:
            copy.wait_send()
        for copy in token_copies:
            copy.wait()

    vmem = pl.BlockSpec(memory_space=pltpu.VMEM)
    given = [block] if tokens is None else [block, tokens]
    shapes = [jax.ShapeDtypeStruct((rows, n * width), block.dtype)]
    scratch = [
        pltpu.SemaphoreType.DMA((32,)),
        pltpu.SemaphoreType.DMA((n, 2)),
        pltpu.SemaphoreType.DMA,
    ]
    if tokens is not None:
        shapes.append(jax.ShapeDtypeStruct((2,) + tokens.shape, tokens.dtype))
        scratch.append(pltpu.SemaphoreType.DMA((2, 2)))
    return pl.pallas_call(
        body,
        out_shape=shapes,
        in_specs=[vmem] * len(given),
        out_specs=[vmem] * len(shapes),
        scratch_shapes=scratch,
        compiler_params=pltpu.CompilerParams(collective_id=cid, has_side_effects=True),
    )(*given)


def ring_scatter(cid, partial, row_part, weight_part):
    pieces = 4
    chip_rows = weight_part.shape[0] // 4
    piece_rows = chip_rows // pieces
    side = weight_part.shape[1] // 2
    rows, columns = partial.shape
    n = lax.axis_size("ch")
    width = columns // n
    half = rows // 2
    step_rows = 32

    def body(
        part, row_in, w_in, out, row_out, w_out, mate, acc, fwd, blk, cross, mine, row_buf, w_one, w_sum, w_two,
        sems, row_send, row_recv, w_sems
    ):
        x, z, core = spot()
        me = place(x, z, core)
        z_up, z_down, z_far = lax.rem(z + 1, 4), lax.rem(z + 3, 4), lax.rem(z + 2, 4)
        up, down = place(x, z_up, core), place(x, z_down, core)
        over, twin = place(1 - x, z, core), place(x, z, 1 - core)
        barrier = pltpu.get_barrier_semaphore()

        def greet(step, carry):
            peer = lax.rem(me + step, n)
            pl.semaphore_signal(barrier, inc=1, device_id={"ch": peer}, device_id_type=MESH)
            return carry

        lax.fori_loop(1, n, greet, 0)
        at_seq = lax.axis_index("seq")
        y, x_low = at_seq // 2, lax.rem(at_seq, 2)
        onward = [lax.rem(y + 1, 4) * 2 + x_low, lax.rem(y + 3, 4) * 2 + x_low]
        for peer in onward:
            pl.semaphore_signal(barrier, inc=1, device_id={"seq": peer}, device_id_type=MESH)
        pl.semaphore_wait(barrier, n + 1)

        def w_own(chunk, way, p):
            first = pl.multiple_of(chunk * chip_rows + p * piece_rows, piece_rows)
            return w_in.at[pl.ds(first, piece_rows), pl.ds(way * side, side)]

        def w_copy(src, dst, step, way, p):
            return pltpu.make_async_remote_copy(
                src_ref=src,
                dst_ref=dst,
                send_sem=w_sems.at[0, step, way, p],
                recv_sem=w_sems.at[1, step, way, p],
                device_id={"seq": onward[way]},
                device_id_type=MESH,
            )

        def behind(way, by):
            return lax.rem(y + (4 - by if way == 0 else by), 4)

        first_step = {}
        second_step = {}
        for p in range(pieces):
            for way in (0, 1):
                copy = w_copy(w_own(behind(way, 1), way, p), w_one.at[way, p], 0, way, p)
                copy.start()
                first_step[way, p] = copy

        def w_add(target, left, right):
            def chunk(i, carry):
                index = pl.ds(pl.multiple_of(i * 16, 16), 16)
                target[index, :] = (left[index, :].astype(f32) + right[index, :].astype(f32)).astype(bf16)
                return carry

            lax.fori_loop(0, piece_rows // 16, chunk, 0)

        def w_first(p):
            for way in (0, 1):
                first_step[way, p].wait_recv()
                w_add(w_sum.at[way, p], w_one.at[way, p], w_own(behind(way, 2), way, p))
                copy = w_copy(w_sum.at[way, p], w_two.at[way, p], 1, way, p)
                copy.start()
                second_step[way, p] = copy

        def w_second(p):
            for way in (0, 1):
                second_step[way, p].wait_recv()
                w_add(
                    w_out.at[way, pl.ds(p * piece_rows, piece_rows), :],
                    w_two.at[way, p],
                    w_own(behind(way, 3), way, p),
                )

        def columns_of(px, pz, pk):
            return pl.ds(pl.multiple_of(place(px, pz, pk) * width, width), width)

        order = []
        for px in (1 - x, x):
            for pz in (z_far, z_up, z_down, z):
                order.append((px, pz))

        def remote(src, dst, k, to):
            return pltpu.make_async_remote_copy(
                src_ref=src,
                dst_ref=dst,
                send_sem=sems.at[0, k],
                recv_sem=sems.at[1, k],
                device_id={"ch": to},
                device_id_type=MESH,
            )

        firsts = []
        for i, (px, pz) in enumerate(order):
            copy = remote(part.at[:, columns_of(px, pz, 1 - core)], mate.at[i], i, twin)
            copy.start()
            firsts.append(copy)

        def row_copy(peer, slot):
            return pltpu.make_async_remote_copy(
                src_ref=row_in,
                dst_ref=row_buf.at[me],
                send_sem=row_send.at[slot],
                recv_sem=row_recv.at[me],
                device_id={"ch": peer},
                device_id_type=MESH,
            )

        def push_row(step, carry):
            row_copy(lax.rem(me + step, n), step).start()
            return carry

        lax.fori_loop(1, n, push_row, 0)

        def add(target, sources, first, size):
            def chunk(i, carry):
                at = pl.ds(pl.multiple_of(first + i * step_rows, step_rows), step_rows)
                total = None
                for ref, base in sources:
                    index = pl.ds(pl.multiple_of(first - base + i * step_rows, step_rows), step_rows)
                    term = ref[index, :].astype(f32)
                    total = term if total is None else total + term
                target[at, :] = total.astype(target.dtype)
                return carry

            lax.fori_loop(0, size // step_rows, chunk, 0)

        def meet(i):
            px, pz = order[i]
            firsts[i].wait_recv()
            add(acc.at[i], ((part.at[:, columns_of(px, pz, core)], 0), (mate.at[i], 0)), 0, rows)

        slots = 8

        def begin(p):
            base = 4 * p
            meet(base)
            k = slots + 4 * p
            a = remote(acc.at[base, pl.ds(0, half), :], fwd.at[p, 0], k, up)
            b = remote(acc.at[base, pl.ds(half, half), :], fwd.at[p, 1], k + 1, down)
            a.start()
            b.start()
            meet(base + 1)
            meet(base + 2)
            meet(base + 3)
            return a, b

        def middle(p, pair):
            base, k = 4 * p, slots + 4 * p
            a, b = pair
            a.wait_recv()
            add(acc.at[base + 1], ((acc.at[base + 1], 0), (fwd.at[p, 0], 0)), 0, half)
            c = remote(acc.at[base + 1], blk.at[p, 0], k + 2, up)
            c.start()
            b.wait_recv()
            add(acc.at[base + 2], ((acc.at[base + 2], 0), (fwd.at[p, 1], half)), half, half)
            d = remote(acc.at[base + 2], blk.at[p, 1], k + 3, down)
            d.start()
            return c, d

        pair = begin(0)
        w_first(0)
        blocks = middle(0, pair)
        w_first(1)
        pair_own = begin(1)
        w_first(2)
        blocks_own = middle(1, pair_own)
        w_first(3)
        for copy in blocks:
            copy.wait_recv()
        add(mine, ((acc.at[3], 0), (blk.at[0, 0], 0), (blk.at[0, 1], 0)), 0, rows)
        crossing = remote(mine, cross, slots + 8, over)
        crossing.start()
        w_second(0)
        w_second(1)
        for copy in blocks_own:
            copy.wait_recv()
        crossing.wait_recv()
        add(out, ((acc.at[7], 0), (blk.at[1, 0], 0), (blk.at[1, 1], 0), (cross, 0)), 0, rows)
        w_second(2)
        w_second(3)
        for copy in [*firsts, *pair, *blocks, *pair_own, *blocks_own, crossing]:
            copy.wait_send()
        for copy in [*first_step.values(), *second_step.values()]:
            copy.wait_send()

        def gather_row(step, carry):
            peer = lax.rem(me + step, n)
            row_copy(peer, step).wait_send()
            pltpu.make_async_remote_copy(
                src_ref=row_in,
                dst_ref=row_buf.at[peer],
                send_sem=row_send.at[step],
                recv_sem=row_recv.at[peer],
                device_id={"ch": peer},
                device_id_type=MESH,
            ).wait_recv()
            return carry + row_buf[peer]

        row_out[...] = lax.fori_loop(1, n, gather_row, row_in[...])

    vmem = pl.BlockSpec(memory_space=pltpu.VMEM)
    return pl.pallas_call(
        body,
        out_shape=[
            jax.ShapeDtypeStruct((rows, width), f32),
            jax.ShapeDtypeStruct(row_part.shape, f32),
            jax.ShapeDtypeStruct((2, chip_rows, side), bf16),
        ],
        in_specs=[vmem] * 3,
        out_specs=[vmem] * 3,
        scratch_shapes=[
            pltpu.VMEM((8, rows, width), bf16),
            pltpu.VMEM((8, rows, width), bf16),
            pltpu.VMEM((2, 2, half, width), bf16),
            pltpu.VMEM((2, 2, rows, width), bf16),
            pltpu.VMEM((rows, width), bf16),
            pltpu.VMEM((rows, width), bf16),
            pltpu.VMEM((n,) + row_part.shape, f32),
            pltpu.VMEM((2, pieces, piece_rows, side), bf16),
            pltpu.VMEM((2, pieces, piece_rows, side), bf16),
            pltpu.VMEM((2, pieces, piece_rows, side), bf16),
            pltpu.SemaphoreType.DMA((2, 17)),
            pltpu.SemaphoreType.DMA((n,)),
            pltpu.SemaphoreType.DMA((n,)),
            pltpu.SemaphoreType.DMA((2, 2, 2, pieces)),
        ],
        compiler_params=pltpu.CompilerParams(collective_id=cid, has_side_effects=True),
    )(partial, row_part, weight_part)


def lag_sum(x, taps):
    tap_count, width = taps.shape
    rows = x.shape[0] - tap_count
    length = rows // SUB
    span = length + tap_count - 1
    group = 11
    tap_group = 8

    def body(x_ref, taps_ref, y_ref, spread, wide):
        for lane in range(width // LANES):
            lanes = slice(lane * LANES, (lane + 1) * LANES)

            def arrange(q, carry):
                spread[q] = x_ref[lane, pl.ds(q, SUB, stride=length), :]
                return carry

            lax.fori_loop(0, span, arrange, 0)

            def widen(k, carry):
                eight = taps_ref[pl.ds(pl.multiple_of(k * SUB, SUB), SUB), lanes]
                for i in range(SUB):
                    wide[k * SUB + i] = jnp.broadcast_to(eight[i : i + 1], (SUB, LANES))
                return carry

            lax.fori_loop(0, tap_count // SUB, widen, 0)

            def block(b, carry):
                first = b * group

                def add(kb, sums):
                    base = first + (tap_count - tap_group) - kb * tap_group
                    window = [spread[base + w] for w in range(group + tap_group - 1)]
                    out = list(sums)
                    for kk in range(tap_group):
                        tap = wide[kb * tap_group + kk]
                        for r in range(group):
                            out[r] = out[r] + tap * window[r + tap_group - 1 - kk]
                    return tuple(out)

                zero = tuple(jnp.zeros((SUB, LANES), f32) for _ in range(group))
                sums = lax.fori_loop(0, tap_count // tap_group, add, zero)
                for r in range(group):
                    y_ref[lane, pl.ds(first + r, SUB, stride=length), :] = sums[r]
                return carry

            lax.fori_loop(0, length // group, block, 0)

    vmem = pl.BlockSpec(memory_space=pltpu.VMEM)
    lanes_first = jnp.stack([x[:, i : i + LANES] for i in range(0, width, LANES)], axis=0)
    y = pl.pallas_call(
        body,
        out_shape=jax.ShapeDtypeStruct((width // LANES, rows, LANES), f32),
        in_specs=[vmem, vmem],
        out_specs=vmem,
        scratch_shapes=[
            pltpu.VMEM((span, SUB, LANES), f32),
            pltpu.VMEM((tap_count, SUB, LANES), f32),
        ],
        name="lag_sum",
    )(lanes_first, taps)
    return jnp.concatenate([y[i] for i in range(width // LANES)], axis=1)


def split_lanes(x):
    return jnp.stack([x[:, i : i + LANES] for i in range(0, x.shape[1], LANES)], axis=0)


def join_lanes(x):
    return jnp.concatenate([x[i] for i in range(x.shape[0])], axis=1)


def mode_close(ahead, behind, rates):
    groups, rows, _ = ahead.shape
    modes, width = rates.shape
    length = rows // SUB
    unroll = 4

    def body(a_ref, b_ref, rate_ref, chunk_ref, shard_ref):
        order = lax.broadcasted_iota(jnp.int32, (SUB, LANES), 0).astype(f32)
        for way, src in enumerate((a_ref, b_ref)):
            for lane in range(groups):
                lanes = slice(lane * LANES, (lane + 1) * LANES)
                rate = [jnp.broadcast_to(rate_ref[m : m + 1, lanes], (SUB, LANES)) for m in range(modes)]
                decay = [jnp.exp(-r) for r in rate]

                def step(i, states):
                    states = list(states)
                    for u in range(unroll):
                        r = i * unroll + u
                        if way == 1:
                            r = length - 1 - r
                        x = src[lane, pl.ds(r, SUB, stride=length), :]
                        states = [decay[m] * states[m] + x for m in range(modes)]
                    return tuple(states)

                zero = tuple(jnp.zeros((SUB, LANES), f32) for _ in range(modes))
                states = lax.fori_loop(0, length // unroll, step, zero)
                after = (SUB - 1) - order if way == 0 else order
                for m in range(modes):
                    chunk_ref[way, m, :, lanes] = states[m]
                    weighted = states[m] * jnp.exp(-(rate[m] * (after * float(length))))
                    shard_ref[way, m : m + 1, lanes] = jnp.sum(weighted, axis=0, keepdims=True)

    vmem = pl.BlockSpec(memory_space=pltpu.VMEM)
    return pl.pallas_call(
        body,
        out_shape=[
            jax.ShapeDtypeStruct((2, modes, SUB, width), f32),
            jax.ShapeDtypeStruct((2, modes, width), f32),
        ],
        in_specs=[vmem] * 3,
        out_specs=[vmem] * 2,
        name="mode_close",
    )(ahead, behind, rates)


def mode_apply(ahead, behind, rates, residues, chunks, entering):
    groups, rows, _ = ahead.shape
    modes, _ = rates.shape
    length = rows // SUB
    unroll = 2

    def body(a_ref, b_ref, rate_ref, res_ref, chunk_ref, enter_ref, ya_ref, yb_ref):
        order = lax.broadcasted_iota(jnp.int32, (SUB, LANES), 0)
        for way, (src, dst) in enumerate(((a_ref, ya_ref), (b_ref, yb_ref))):
            place = order if way == 0 else (SUB - 1) - order
            for lane in range(groups):
                lanes = slice(lane * LANES, (lane + 1) * LANES)
                decay = []
                residue = []
                start = []
                for m in range(modes):
                    rate = jnp.broadcast_to(rate_ref[m : m + 1, lanes], (SUB, LANES))
                    decay.append(jnp.exp(-rate))
                    residue.append(jnp.broadcast_to(res_ref[m : m + 1, lanes], (SUB, LANES)))
                    first = jnp.broadcast_to(enter_ref[way, m : m + 1, lanes], (SUB, LANES))

                    def back(v, by):
                        moved = pltpu.roll(v, by if way == 0 else SUB - by, 0)
                        return moved

                    state = jnp.where(place == 0, first, back(chunk_ref[way, m, :, lanes], 1))
                    for by in (1, 2, 4):
                        factor = jnp.exp(-(rate * float(by * length)))
                        state = state + jnp.where(place >= by, factor * back(state, by), 0.0)
                    start.append(state)

                def step(i, states):
                    states = list(states)
                    for u in range(unroll):
                        r = i * unroll + u
                        if way == 1:
                            r = length - 1 - r
                        x = src[lane, pl.ds(r, SUB, stride=length), :]
                        states = [decay[m] * states[m] + x for m in range(modes)]
                        terms = [residue[m] * states[m] for m in range(modes)]
                        while len(terms) > 1:
                            terms = [a + b for a, b in zip(terms[::2], terms[1::2])]
                        dst[lane, pl.ds(r, SUB, stride=length), :] = terms[0]
                    return tuple(states)

                lax.fori_loop(0, length // unroll, step, tuple(start))

    vmem = pl.BlockSpec(memory_space=pltpu.VMEM)
    return pl.pallas_call(
        body,
        out_shape=[jax.ShapeDtypeStruct(ahead.shape, f32)] * 2,
        in_specs=[vmem] * 6,
        out_specs=[vmem] * 2,
        name="mode_apply",
    )(ahead, behind, rates, residues, chunks, entering)


def shift_axis(shard, axis, by):
    n = lax.axis_size(axis)
    pairs = [(i, i + by) for i in range(n) if 0 <= i + by < n]
    return lax.ppermute(shard, axis, pairs)


def taps_ahead(projected, short_filter, first, rows):
    tap_count = short_filter.shape[0]
    running = None
    for i in range(tap_count):
        term = short_filter[i] * projected[first - i : first - i + rows].astype(f32)
        running = term if running is None else running + term
    return running


def taps_behind(gradient, short_filter, rows):
    running = None
    for i in range(short_filter.shape[0]):
        term = short_filter[i] * gradient[i : i + rows].astype(f32)
        running = term if running is None else running + term
    return running


def normalise(whole, gain):
    as_float = whole.astype(f32)
    scale = lax.rsqrt(jnp.mean(as_float * as_float, axis=1) + epsilon)
    return (as_float * scale[:, None] * gain[None, :].astype(f32)).astype(bf16), scale


def last_ring_step(ring_sums, weight_part):
    at = lax.axis_index("seq")
    y, x_low = at // 2, lax.rem(at, 2)
    n_seq = lax.axis_size("seq")
    chip_rows = ring_sums.shape[1]
    arrived = [
        lax.ppermute(
            ring_sums[way], "seq", [(k, (k // 2 + step) % 4 * 2 + k % 2) for k in range(n_seq)]
        )
        for way, step in ((0, 1), (1, 3))
    ]
    own = lax.dynamic_slice_in_dim(weight_part, y * chip_rows, chip_rows, 0)
    sums = jnp.concatenate(arrived, axis=1).astype(f32) + own.astype(f32)
    part = chip_rows // 2
    theirs = lax.dynamic_slice_in_dim(sums, (1 - x_low) * part, part, 0).astype(bf16)
    return lax.dynamic_slice_in_dim(sums, x_low * part, part, 0), theirs


def cross(theirs):
    return lax.ppermute(theirs, "seq", [(k, k ^ 1) for k in range(lax.axis_size("seq"))]).astype(f32)


def small(vector, lanes=LANES):
    rows = vector.reshape(-1, lanes)
    pad = -rows.shape[0] % SUB
    return jnp.pad(rows, ((0, pad), (0, 0)))


def per_device(
    token_ids,
    embedding,
    gain_first,
    gain_second,
    weights_first,
    weights_second,
    short_first,
    short_second,
    medium,
    residues,
    decay_rates,
    cotangent,
):
    n_seq = lax.axis_size("seq")
    seq_at = lax.axis_index("seq")
    rows = token_ids.shape[0]
    vocab, width = embedding.shape
    features = weights_first.shape[0]
    wide = 3 * width
    vocab_part = vocab // n_seq
    flat_first = weights_first.reshape(features, wide)
    flat_second = weights_second.reshape(features, wide)
    taps_first = short_first.reshape(-1, wide)
    taps_second = short_second.reshape(-1, wide)

    packed = jnp.concatenate(
        [embedding, gain_first[None], gain_second[None], jnp.zeros((14, width), bf16)], axis=0
    )
    joined, around = ring_gather(0, packed, small(token_ids))
    before = jnp.where(seq_at == 0, -1, around[0].reshape(-1)[rows - HALO : rows])
    after = jnp.where(seq_at == n_seq - 1, -1, around[1].reshape(-1)[:HALO])
    ids = jnp.concatenate([before, token_ids, after])
    whole_gain_first, whole_gain_second = joined[vocab], joined[vocab + 1]
    table_normed, table_scale = normalise(joined[:vocab], whole_gain_first)
    table_projected = jnp.dot(table_normed, flat_first, preferred_element_type=f32).astype(bf16)
    table = jnp.concatenate([table_projected, embedding], axis=1)

    onehot = (ids[:, None] == jnp.arange(vocab, dtype=jnp.int32)[None, :]).astype(bf16)
    looked_up = jnp.dot(onehot, table, preferred_element_type=f32).astype(bf16)
    ahead = HALO - SUB
    featured_first = taps_ahead(looked_up[:, :wide], taps_first, SUB, looked_up.shape[0] - SUB)
    gated_first = (
        (featured_first[:, width : 2 * width] * featured_first[:, 2 * width :]).astype(bf16).astype(f32)
    )
    medium_float = medium.astype(f32)
    tap_count = medium.shape[0]
    out_rows = rows + 2 * LEAD
    begin = ahead - LEAD - (tap_count - 1)
    filtered_first = lag_sum(gated_first[begin : begin + out_rows + tap_count], medium_float)
    near = slice(ahead - LEAD, ahead - LEAD + out_rows)
    embedded = looked_up[HALO - LEAD : HALO - LEAD + out_rows, wide:].astype(f32)
    middle_near = (embedded + featured_first[near, :width] * filtered_first).astype(bf16)
    middle = middle_near[LEAD : LEAD + rows]

    whole_rows = ring_gather(1, middle_near)[0]
    normed_near, scale_near = normalise(whole_rows, whole_gain_second)
    normed_second, scale_second = normed_near[LEAD : LEAD + rows], scale_near[LEAD : LEAD + rows]
    projected_near = jnp.dot(normed_near, flat_second, preferred_element_type=f32).astype(bf16)
    featured_second = taps_ahead(projected_near, taps_second, LEAD, rows)
    pick = [featured_second[:, j * width : (j + 1) * width] for j in range(3)]
    gated_second = (pick[1] * pick[2]).astype(bf16).astype(f32)
    above_second = cotangent.astype(f32)
    grad_filtered = (above_second * pick[0]).astype(bf16).astype(f32)
    gated_lanes, grad_lanes = split_lanes(gated_second), split_lanes(grad_filtered)
    chunks, shard_states = mode_close(gated_lanes, grad_lanes, decay_rates)
    (all_states,) = exchange(2, [Item(shard_states, "seq", window="onward")])
    other = jnp.arange(n_seq, dtype=jnp.int32)
    gaps = jnp.stack([seq_at - 1 - other, other - 1 - seq_at], axis=1)
    all_states = all_states[:, None]
    weights_of = jnp.where(
        (gaps >= 0)[:, :, None, None],
        jnp.exp(-decay_rates[None, None] * (jnp.maximum(gaps, 0) * rows).astype(f32)[:, :, None, None]),
        0.0,
    )
    entering = jnp.sum(weights_of * all_states, axis=0)
    filtered_lanes, gated_grad_lanes = mode_apply(
        gated_lanes, grad_lanes, decay_rates, residues, chunks, entering
    )
    filtered_second, grad_gated = join_lanes(filtered_lanes), join_lanes(gated_grad_lanes)
    output = (middle.astype(f32) + pick[0] * filtered_second).astype(bf16)

    grad_featured = jnp.concatenate(
        [above_second * filtered_second, grad_gated * pick[2], grad_gated * pick[1]], axis=1
    ).astype(bf16)
    following = shift_axis(grad_featured[:SUB], "seq", -1)
    grad_projected = taps_behind(
        jnp.concatenate([grad_featured, following], axis=0), taps_second, rows
    ).astype(bf16)
    row_part = jnp.sum(
        grad_projected.astype(f32) * projected_near[LEAD : LEAD + rows].astype(f32), axis=1
    )
    partial_sum = lax.dot_general(
        grad_projected, flat_second, (((1,), (1,)), ((), ())), preferred_element_type=f32
    ).astype(bf16)
    weight_part = lax.dot_general(
        normed_second, grad_projected, (((0,), (0,)), ((), ())), preferred_element_type=f32
    ).astype(bf16)
    grad_normed, row_total, ring_sums = ring_scatter(3, partial_sum, small(row_part), weight_part)
    ours, theirs = last_ring_step(ring_sums, weight_part)
    row_total = row_total.reshape(-1)[:rows]
    middle_float = middle.astype(f32)
    scale = scale_second[:, None]
    grad_middle = (
        above_second
        + scale * grad_normed * gain_second.astype(f32)
        - middle_float * (scale * scale) * row_total[:, None] / features
    ).astype(bf16)
    gain_part_second = jnp.sum(grad_normed * middle_float * scale, axis=0)

    grad_near = jnp.concatenate([grad_middle, shift_axis(grad_middle[:HALO], "seq", -1)], axis=0)
    from_here = slice(ahead, ahead + rows + HALO)
    grad_filtered = (
        (grad_near.astype(f32) * featured_first[from_here, :width]).astype(bf16).astype(f32)
    )
    grad_gated = lag_sum(grad_filtered, medium_float[::-1])[: rows + SUB]
    here = slice(ahead, ahead + rows + SUB)
    grad_featured = jnp.concatenate(
        [
            grad_near[: rows + SUB].astype(f32) * filtered_first[LEAD:],
            grad_gated * featured_first[here, 2 * width :],
            grad_gated * featured_first[here, width : 2 * width],
        ],
        axis=1,
    ).astype(bf16)
    grad_projected = taps_behind(grad_featured, taps_first, rows).astype(bf16)
    by_token = lax.dot_general(
        onehot[HALO : HALO + rows],
        jnp.concatenate([grad_projected, grad_middle], axis=1),
        (((0,), (0,)), ((), ())),
        preferred_element_type=f32,
    ).astype(bf16)
    by_token, theirs = lax.optimization_barrier((by_token, theirs))
    crossed = cross(theirs)
    (token_sums,) = exchange(4, [Item(by_token, "seq", window=0, reduce=True)])
    weight_grad_second = ours + crossed
    token_grad = token_sums[:, :wide].astype(bf16)
    token_above = token_sums[:, wide:]
    own_part = lambda array: lax.dynamic_slice_in_dim(array, seq_at * vocab_part, vocab_part, 0)
    token_part = jnp.sum(token_grad.astype(f32) * own_part(table_projected).astype(f32), axis=1)
    token_partial = lax.dot_general(
        token_grad, flat_first, (((1,), (1,)), ((), ())), preferred_element_type=f32
    ).astype(bf16)
    spread = jnp.broadcast_to(token_part[:, None], (vocab_part, LANES))
    token_normed, token_total, token_grads = exchange(
        5,
        [
            Item(token_partial, "ch", window=1, reduce=True),
            Item(spread, "ch", reduce=True),
            Item(token_grad, "seq"),
        ],
    )
    table_float = own_part(embedding).astype(f32)
    scale = own_part(table_scale)[:, None]
    grad_table = (
        token_above
        + scale * token_normed * gain_first.astype(f32)
        - table_float * (scale * scale) * token_total[:, :1] / features
    )
    gain_part_first = jnp.sum(token_normed * table_float * scale, axis=0)
    gain_parts = jnp.concatenate(
        [gain_part_first[None], gain_part_second[None], jnp.zeros((6, width), f32)], axis=0
    )
    table_parts, gain_total = exchange(
        6, [Item(grad_table.astype(bf16), "seq"), Item(gain_parts, "seq", reduce=True)]
    )
    weight_grad_first = lax.dot_general(
        lax.dynamic_slice_in_dim(table_normed, seq_at * (features // n_seq), features // n_seq, 1),
        token_grads.reshape(vocab, wide),
        (((0,), (0,)), ((), ())),
        preferred_element_type=f32,
    )
    return (
        output,
        table_parts.reshape(vocab, width).astype(f32),
        gain_total[0],
        gain_total[1],
        weight_grad_first.reshape(-1, 3, width),
        weight_grad_second.reshape(-1, 3, width),
    )


def solution(mesh):
    placed = (
        P("seq"),
        P(None, "ch"),
        P("ch"),
        P("ch"),
        P(None, None, "ch"),
        P(None, None, "ch"),
        P(None, None, "ch"),
        P(None, None, "ch"),
        P(None, "ch"),
        P(None, "ch"),
        P(None, "ch"),
        P("seq", "ch"),
    )
    return jax.shard_map(
        per_device,
        mesh=mesh,
        in_specs=placed,
        out_specs=(
            P("seq", "ch"),
            P(None, "ch"),
            P("ch"),
            P("ch"),
            P("seq", None, "ch"),
            P("seq", None, "ch"),
        ),
        check_vma=False,
    )
```

```python
import jax
import jax.numpy as jnp
from jax import lax
from jax.experimental import pallas as pl
from jax.experimental.pallas import tpu as pltpu
from jax.sharding import PartitionSpec as P


epsilon = 1e-06
MESH = pl.DeviceIdType.MESH
f32 = jnp.float32
bf16 = jnp.bfloat16
LANES = 128
SUB = 8
HALO = 144
LEAD = 8


class Item:
    def __init__(self, array, axis, window=None, reduce=False):
        self.array, self.axis, self.window, self.reduce = array, axis, window, reduce

    def block(self):
        shape = list(self.array.shape)
        if self.window == "onward":
            return tuple(shape[1:])
        if self.window is not None:
            shape[self.window] //= lax.axis_size(self.axis)
        return tuple(shape)


def exchange(cid, items):
    count = len(items)
    sizes = [lax.axis_size(it.axis) for it in items]
    blocks = [it.block() for it in items]
    axes = []
    for it in items:
        if it.axis not in axes:
            axes.append(it.axis)
    most = max(sizes)
    reduced = [k for k in range(count) if items[k].reduce]

    def body(*refs):
        srcs, outs = refs[:count], refs[count : 2 * count]
        bufs = list(outs)
        rest = refs[2 * count :]
        for slot, k in enumerate(reduced):
            bufs[k] = rest[slot]
        send_sem, recv_sem, own_sem = rest[len(reduced) :]

        def part(k, peer):
            if items[k].window is None:
                return srcs[k]
            if items[k].window == "onward":
                return srcs[k].at[jnp.where(peer > lax.axis_index(items[k].axis), 0, 1)]
            width = blocks[k][items[k].window]
            start = pl.multiple_of(peer * width, width)
            index = [slice(None)] * len(blocks[k])
            index[items[k].window] = pl.ds(start, width)
            return srcs[k].at[tuple(index)]

        barrier = pltpu.get_barrier_semaphore()
        total = 0
        for axis in axes:
            n = lax.axis_size(axis)
            total += n - 1
            me = lax.axis_index(axis)

            def greet(step, carry, axis=axis, n=n, me=me):
                peer = lax.rem(me + step, n)
                pl.semaphore_signal(barrier, inc=1, device_id={axis: peer}, device_id_type=MESH)
                return carry

            lax.fori_loop(1, n, greet, 0)
        pl.semaphore_wait(barrier, total)

        def copy(k, peer, slot):
            me = lax.axis_index(items[k].axis)
            return pltpu.make_async_remote_copy(
                src_ref=part(k, peer),
                dst_ref=bufs[k].at[me],
                send_sem=send_sem.at[k, slot],
                recv_sem=recv_sem.at[k, me],
                device_id={items[k].axis: peer},
                device_id_type=MESH,
            )

        for k in range(count):
            n = sizes[k]
            me = lax.axis_index(items[k].axis)

            def push(step, carry, k=k, n=n, me=me):
                copy(k, lax.rem(me + step, n), step).start()
                return carry

            lax.fori_loop(1, n, push, 0)
        for k in range(count):
            me = lax.axis_index(items[k].axis)
            pltpu.make_async_copy(part(k, me), bufs[k].at[me], own_sem.at[k]).start()
        for k in range(count):
            n = sizes[k]
            me = lax.axis_index(items[k].axis)
            pltpu.make_async_copy(part(k, me), bufs[k].at[me], own_sem.at[k]).wait()

            def finish(step, carry, k=k, n=n, me=me):
                peer = lax.rem(me + step, n)
                copy(k, peer, step).wait_send()
                pltpu.make_async_remote_copy(
                    src_ref=part(k, peer),
                    dst_ref=bufs[k].at[peer],
                    send_sem=send_sem.at[k, step],
                    recv_sem=recv_sem.at[k, peer],
                    device_id={items[k].axis: peer},
                    device_id_type=MESH,
                ).wait_recv()
                return carry

            lax.fori_loop(1, n, finish, 0)
            if items[k].reduce:
                running = bufs[k][0].astype(f32)
                for j in range(1, n):
                    running = running + bufs[k][j].astype(f32)
                outs[k][...] = running

    shapes = []
    scratch = []
    for k in range(count):
        full = (sizes[k],) + blocks[k]
        if items[k].reduce:
            shapes.append(jax.ShapeDtypeStruct(blocks[k], f32))
            scratch.append(pltpu.VMEM(full, items[k].array.dtype))
        else:
            shapes.append(jax.ShapeDtypeStruct(full, items[k].array.dtype))
    scratch += [
        pltpu.SemaphoreType.DMA((count, most)),
        pltpu.SemaphoreType.DMA((count, most)),
        pltpu.SemaphoreType.DMA((count,)),
    ]
    vmem = pl.BlockSpec(memory_space=pltpu.VMEM)
    return pl.pallas_call(
        body,
        out_shape=shapes,
        in_specs=[vmem] * count,
        out_specs=[vmem] * count,
        scratch_shapes=scratch,
        compiler_params=pltpu.CompilerParams(collective_id=cid, has_side_effects=True),
    )(*[it.array for it in items])


def place(axis, plane, ring, core):
    return plane * 8 + ring * 2 + core if axis == "ch" else ring * 2 + plane


def spot(axis):
    at = lax.axis_index(axis)
    if axis == "ch":
        return at // 8, lax.rem(at // 2, 4), lax.rem(at, 2)
    return lax.rem(at, 2), at // 2, 0


def ring_gather(cid, axis, block, tokens=None):
    rows, width = block.shape
    n = lax.axis_size(axis)
    twins = axis == "ch"
    cut = (rows // 2 + 15) // 16 * 16
    halves = ((0, cut), (cut, rows - cut))

    def body(*refs):
        if tokens is None:
            src, out, send_sem, recv_sem, own_sem = refs
        else:
            src, token_in, out, token_out, send_sem, recv_sem, own_sem, token_sem = refs
        x, z, core = spot(axis)
        me = place(axis, x, z, core)
        z_up, z_down, z_far = lax.rem(z + 1, 4), lax.rem(z + 3, 4), lax.rem(z + 2, 4)
        up, down, far = (place(axis, x, to, core) for to in (z_up, z_down, z_far))
        over, twin = place(axis, 1 - x, z, core), place(axis, x, z, 1 - core)
        over_up, over_down, over_far = (place(axis, 1 - x, to, core) for to in (z_up, z_down, z_far))

        barrier = pltpu.get_barrier_semaphore()
        peers = [up, down, over] + ([twin] if twins else [])
        for peer in peers:
            pl.semaphore_signal(barrier, inc=1, device_id={axis: peer}, device_id_type=MESH)
        token_copies = []
        if tokens is None:
            pl.semaphore_wait(barrier, len(peers))
        else:
            shards = lax.axis_size("seq")
            at = lax.axis_index("seq")
            for slot, peer in ((0, lax.rem(at + 1, shards)), (1, lax.rem(at + shards - 1, shards))):
                pl.semaphore_signal(barrier, inc=1, device_id={"seq": peer}, device_id_type=MESH)
                token_copies.append(
                    pltpu.make_async_remote_copy(
                        src_ref=token_in,
                        dst_ref=token_out.at[slot],
                        send_sem=token_sem.at[0, slot],
                        recv_sem=token_sem.at[1, slot],
                        device_id={"seq": peer},
                        device_id_type=MESH,
                    )
                )
            pl.semaphore_wait(barrier, len(peers) + 2)

        def window(c, h):
            first, size = halves[h]
            if not twins:
                return out.at[c, pl.ds(first, size), :]
            return out.at[pl.ds(first, size), pl.ds(pl.multiple_of(c * width, width), width)]

        sends = []

        def send(c, h, to, ref=None):
            copy = pltpu.make_async_remote_copy(
                src_ref=window(c, h) if ref is None else ref,
                dst_ref=window(c, h),
                send_sem=send_sem.at[len(sends)],
                recv_sem=recv_sem.at[c, h],
                device_id={axis: to},
                device_id_type=MESH,
            )
            copy.start()
            sends.append(copy)

        def share(c, h, ref=None):
            if twins:
                send(c, h, twin, ref)

        def arrive(c, h):
            pltpu.make_async_remote_copy(
                src_ref=window(c, h),
                dst_ref=window(c, h),
                send_sem=send_sem.at[0],
                recv_sem=recv_sem.at[c, h],
                device_id={axis: over},
                device_id_type=MESH,
            ).wait_recv()

        mine = [src.at[pl.ds(first, size), :] for first, size in halves]
        for h, to in ((0, up), (1, down), (0, over), (1, over), (1, up), (0, down)):
            send(me, h, to, mine[h])
        for h in (0, 1):
            share(me, h, mine[h])
        here = out.at[:, pl.ds(pl.multiple_of(me * width, width), width)] if twins else out.at[me]
        own = pltpu.make_async_copy(src, here, own_sem)
        own.start()
        for copy in token_copies:
            copy.start()
        arrive(down, 0)
        send(down, 0, up)
        arrive(up, 1)
        send(up, 1, down)
        share(down, 0)
        share(up, 1)
        for h in (0, 1):
            arrive(over, h)
            send(over, h, up)
            send(over, h, down)
            share(over, h)
        arrive(down, 1)
        share(down, 1)
        arrive(up, 0)
        share(up, 0)
        arrive(over_down, 0)
        send(over_down, 0, up)
        arrive(over_up, 1)
        send(over_up, 1, down)
        for h in (0, 1):
            arrive(far, h)
            share(far, h)
        share(over_down, 0)
        share(over_up, 1)
        for c, h in ((over_down, 1), (over_up, 0), (over_far, 0), (over_far, 1)):
            arrive(c, h)
            share(c, h)
        if twins:
            for px in (0, 1):
                for pz in range(4):
                    for h in (0, 1):
                        arrive(place(axis, px, pz, 1 - core), h)
        own.wait()
        for copy in sends:
            copy.wait_send()
        for copy in token_copies:
            copy.wait()

    vmem = pl.BlockSpec(memory_space=pltpu.VMEM)
    given = [block] if tokens is None else [block, tokens]
    whole = (rows, n * width) if twins else (n, rows, width)
    shapes = [jax.ShapeDtypeStruct(whole, block.dtype)]
    scratch = [
        pltpu.SemaphoreType.DMA((32,)),
        pltpu.SemaphoreType.DMA((n, 2)),
        pltpu.SemaphoreType.DMA,
    ]
    if tokens is not None:
        shapes.append(jax.ShapeDtypeStruct((2,) + tokens.shape, tokens.dtype))
        scratch.append(pltpu.SemaphoreType.DMA((2, 2)))
    return pl.pallas_call(
        body,
        out_shape=shapes,
        in_specs=[vmem] * len(given),
        out_specs=[vmem] * len(shapes),
        scratch_shapes=scratch,
        compiler_params=pltpu.CompilerParams(collective_id=cid, has_side_effects=True),
    )(*given)


def ring_scatter(cid, axis, partial, row_part=None, weight_part=None):
    n = lax.axis_size(axis)
    twins = axis == "ch"
    rows, width = (partial.shape[0], partial.shape[1] // n) if twins else (partial.shape[0] // n, partial.shape[1])
    half = rows // 2
    step_rows = 32
    has_rows, has_weights = row_part is not None, weight_part is not None
    pieces = 4
    if has_weights:
        chip_rows = weight_part.shape[0] // 4
        piece_rows = chip_rows // pieces
        side = weight_part.shape[1] // 2

    def body(*refs):
        refs = list(refs)
        part = refs.pop(0)
        row_in = refs.pop(0) if has_rows else None
        w_in = refs.pop(0) if has_weights else None
        out = refs.pop(0)
        row_out = refs.pop(0) if has_rows else None
        w_out = refs.pop(0) if has_weights else None
        acc, fwd, blk, cross, mine, sems = refs[:6]
        refs = refs[6:]
        mate = refs.pop(0) if twins else None
        if has_rows:
            row_buf, row_send, row_recv = refs[:3]
            refs = refs[3:]
        if has_weights:
            w_one, w_sum, w_two, w_sems = refs
        x, z, core = spot(axis)
        me = place(axis, x, z, core)
        z_up, z_down, z_far = lax.rem(z + 1, 4), lax.rem(z + 3, 4), lax.rem(z + 2, 4)
        up, down = place(axis, x, z_up, core), place(axis, x, z_down, core)
        over, twin = place(axis, 1 - x, z, core), place(axis, x, z, 1 - core)
        barrier = pltpu.get_barrier_semaphore()
        if has_rows:

            def greet(step, carry):
                peer = lax.rem(me + step, n)
                pl.semaphore_signal(barrier, inc=1, device_id={axis: peer}, device_id_type=MESH)
                return carry

            lax.fori_loop(1, n, greet, 0)
            greeted = n - 1
        else:
            peers = [up, down, over] + ([twin] if twins else [])
            for peer in peers:
                pl.semaphore_signal(barrier, inc=1, device_id={axis: peer}, device_id_type=MESH)
            greeted = len(peers)
        if has_weights:
            at_seq = lax.axis_index("seq")
            y, x_low = at_seq // 2, lax.rem(at_seq, 2)
            onward = [lax.rem(y + 1, 4) * 2 + x_low, lax.rem(y + 3, 4) * 2 + x_low]
            for peer in onward:
                pl.semaphore_signal(barrier, inc=1, device_id={"seq": peer}, device_id_type=MESH)
            greeted += 2
        pl.semaphore_wait(barrier, greeted)

        first_step = {}
        second_step = {}

        def w_own(chunk, way, p):
            first = pl.multiple_of(chunk * chip_rows + p * piece_rows, piece_rows)
            return w_in.at[pl.ds(first, piece_rows), pl.ds(way * side, side)]

        def w_copy(src, dst, step, way, p):
            return pltpu.make_async_remote_copy(
                src_ref=src,
                dst_ref=dst,
                send_sem=w_sems.at[0, step, way, p],
                recv_sem=w_sems.at[1, step, way, p],
                device_id={"seq": onward[way]},
                device_id_type=MESH,
            )

        def behind(way, by):
            return lax.rem(y + (4 - by if way == 0 else by), 4)

        def w_add(target, left, right):
            def chunk(i, carry):
                index = pl.ds(pl.multiple_of(i * 16, 16), 16)
                target[index, :] = (left[index, :].astype(f32) + right[index, :].astype(f32)).astype(bf16)
                return carry

            lax.fori_loop(0, piece_rows // 16, chunk, 0)

        def w_first(p):
            for way in (0, 1) if has_weights else ():
                first_step[way, p].wait_recv()
                w_add(w_sum.at[way, p], w_one.at[way, p], w_own(behind(way, 2), way, p))
                copy = w_copy(w_sum.at[way, p], w_two.at[way, p], 1, way, p)
                copy.start()
                second_step[way, p] = copy

        def w_second(p):
            for way in (0, 1) if has_weights else ():
                second_step[way, p].wait_recv()
                w_add(
                    w_out.at[way, pl.ds(p * piece_rows, piece_rows), :],
                    w_two.at[way, p],
                    w_own(behind(way, 3), way, p),
                )

        for p in range(pieces) if has_weights else ():
            for way in (0, 1):
                copy = w_copy(w_own(behind(way, 1), way, p), w_one.at[way, p], 0, way, p)
                copy.start()
                first_step[way, p] = copy

        def own_block(px, pz, pk):
            at = place(axis, px, pz, pk)
            if twins:
                return part.at[:, pl.ds(pl.multiple_of(at * width, width), width)]
            return part.at[pl.ds(pl.multiple_of(at * rows, rows), rows), :]

        order = []
        for px in (1 - x, x):
            for pz in (z_far, z_up, z_down, z):
                order.append((px, pz))

        def remote(src, dst, k, to):
            return pltpu.make_async_remote_copy(
                src_ref=src,
                dst_ref=dst,
                send_sem=sems.at[0, k],
                recv_sem=sems.at[1, k],
                device_id={axis: to},
                device_id_type=MESH,
            )

        firsts = []
        for i, (px, pz) in enumerate(order) if twins else ():
            copy = remote(own_block(px, pz, 1 - core), mate.at[i], i, twin)
            copy.start()
            firsts.append(copy)

        def row_copy(peer, slot):
            return pltpu.make_async_remote_copy(
                src_ref=row_in,
                dst_ref=row_buf.at[me],
                send_sem=row_send.at[slot],
                recv_sem=row_recv.at[me],
                device_id={axis: peer},
                device_id_type=MESH,
            )

        def push_row(step, carry):
            row_copy(lax.rem(me + step, n), step).start()
            return carry

        if has_rows:
            lax.fori_loop(1, n, push_row, 0)

        def add(target, sources, first, size):
            def chunk(i, carry):
                at = pl.ds(pl.multiple_of(first + i * step_rows, step_rows), step_rows)
                total = None
                for ref, base in sources:
                    index = pl.ds(pl.multiple_of(first - base + i * step_rows, step_rows), step_rows)
                    term = ref[index, :].astype(f32)
                    total = term if total is None else total + term
                target[at, :] = total.astype(target.dtype)
                return carry

            lax.fori_loop(0, size // step_rows, chunk, 0)

        def meet(i):
            px, pz = order[i]
            sources = ((own_block(px, pz, core), 0),)
            if twins:
                firsts[i].wait_recv()
                sources += ((mate.at[i], 0),)
            add(acc.at[i], sources, 0, rows)

        slots = 8

        def begin(p):
            base = 4 * p
            meet(base)
            k = slots + 4 * p
            a = remote(acc.at[base, pl.ds(0, half), :], fwd.at[p, 0], k, up)
            b = remote(acc.at[base, pl.ds(half, half), :], fwd.at[p, 1], k + 1, down)
            a.start()
            b.start()
            meet(base + 1)
            meet(base + 2)
            meet(base + 3)
            return a, b

        def middle(p, pair):
            base, k = 4 * p, slots + 4 * p
            a, b = pair
            a.wait_recv()
            add(acc.at[base + 1], ((acc.at[base + 1], 0), (fwd.at[p, 0], 0)), 0, half)
            c = remote(acc.at[base + 1], blk.at[p, 0], k + 2, up)
            c.start()
            b.wait_recv()
            add(acc.at[base + 2], ((acc.at[base + 2], 0), (fwd.at[p, 1], half)), half, half)
            d = remote(acc.at[base + 2], blk.at[p, 1], k + 3, down)
            d.start()
            return c, d

        pair = begin(0)
        w_first(0)
        blocks = middle(0, pair)
        w_first(1)
        pair_own = begin(1)
        w_first(2)
        blocks_own = middle(1, pair_own)
        w_first(3)
        for copy in blocks:
            copy.wait_recv()
        add(mine, ((acc.at[3], 0), (blk.at[0, 0], 0), (blk.at[0, 1], 0)), 0, rows)
        crossing = remote(mine, cross, slots + 8, over)
        crossing.start()
        w_second(0)
        w_second(1)
        for copy in blocks_own:
            copy.wait_recv()
        crossing.wait_recv()
        add(out, ((acc.at[7], 0), (blk.at[1, 0], 0), (blk.at[1, 1], 0), (cross, 0)), 0, rows)
        w_second(2)
        w_second(3)
        for copy in [*firsts, *pair, *blocks, *pair_own, *blocks_own, crossing]:
            copy.wait_send()
        for copy in [*first_step.values(), *second_step.values()]:
            copy.wait_send()

        def gather_row(step, carry):
            peer = lax.rem(me + step, n)
            row_copy(peer, step).wait_send()
            pltpu.make_async_remote_copy(
                src_ref=row_in,
                dst_ref=row_buf.at[peer],
                send_sem=row_send.at[step],
                recv_sem=row_recv.at[peer],
                device_id={axis: peer},
                device_id_type=MESH,
            ).wait_recv()
            return carry + row_buf[peer]

        if has_rows:
            row_out[...] = lax.fori_loop(1, n, gather_row, row_in[...])

    vmem = pl.BlockSpec(memory_space=pltpu.VMEM)
    given = [partial]
    shapes = [jax.ShapeDtypeStruct((rows, width), f32)]
    scratch = [
        pltpu.VMEM((8, rows, width), bf16),
        pltpu.VMEM((2, 2, half, width), bf16),
        pltpu.VMEM((2, 2, rows, width), bf16),
        pltpu.VMEM((rows, width), bf16),
        pltpu.VMEM((rows, width), bf16),
        pltpu.SemaphoreType.DMA((2, 17)),
    ]
    if twins:
        scratch.append(pltpu.VMEM((8, rows, width), bf16))
    if has_rows:
        given.append(row_part)
        shapes.append(jax.ShapeDtypeStruct(row_part.shape, f32))
        scratch += [
            pltpu.VMEM((n,) + row_part.shape, f32),
            pltpu.SemaphoreType.DMA((n,)),
            pltpu.SemaphoreType.DMA((n,)),
        ]
    if has_weights:
        given.append(weight_part)
        shapes.append(jax.ShapeDtypeStruct((2, chip_rows, side), bf16))
        scratch += [pltpu.VMEM((2, pieces, piece_rows, side), bf16)] * 3
        scratch.append(pltpu.SemaphoreType.DMA((2, 2, 2, pieces)))
    return pl.pallas_call(
        body,
        out_shape=shapes,
        in_specs=[vmem] * len(given),
        out_specs=[vmem] * len(shapes),
        scratch_shapes=scratch,
        compiler_params=pltpu.CompilerParams(collective_id=cid, has_side_effects=True),
    )(*given)


def lag_sum(x, taps):
    tap_count, width = taps.shape
    rows = x.shape[0] - tap_count
    length = rows // SUB
    span = length + tap_count - 1
    group = 11
    tap_group = 8

    def body(x_ref, taps_ref, y_ref, spread, wide):
        for lane in range(width // LANES):
            lanes = slice(lane * LANES, (lane + 1) * LANES)

            def arrange(q, carry):
                spread[q] = x_ref[lane, pl.ds(q, SUB, stride=length), :]
                return carry

            lax.fori_loop(0, span, arrange, 0)

            def widen(k, carry):
                eight = taps_ref[pl.ds(pl.multiple_of(k * SUB, SUB), SUB), lanes]
                for i in range(SUB):
                    wide[k * SUB + i] = jnp.broadcast_to(eight[i : i + 1], (SUB, LANES))
                return carry

            lax.fori_loop(0, tap_count // SUB, widen, 0)

            def block(b, carry):
                first = b * group

                def add(kb, sums):
                    base = first + (tap_count - tap_group) - kb * tap_group
                    window = [spread[base + w] for w in range(group + tap_group - 1)]
                    out = list(sums)
                    for kk in range(tap_group):
                        tap = wide[kb * tap_group + kk]
                        for r in range(group):
                            out[r] = out[r] + tap * window[r + tap_group - 1 - kk]
                    return tuple(out)

                zero = tuple(jnp.zeros((SUB, LANES), f32) for _ in range(group))
                sums = lax.fori_loop(0, tap_count // tap_group, add, zero)
                for r in range(group):
                    y_ref[lane, pl.ds(first + r, SUB, stride=length), :] = sums[r]
                return carry

            lax.fori_loop(0, length // group, block, 0)

    vmem = pl.BlockSpec(memory_space=pltpu.VMEM)
    lanes_first = jnp.stack([x[:, i : i + LANES] for i in range(0, width, LANES)], axis=0)
    y = pl.pallas_call(
        body,
        out_shape=jax.ShapeDtypeStruct((width // LANES, rows, LANES), f32),
        in_specs=[vmem, vmem],
        out_specs=vmem,
        scratch_shapes=[
            pltpu.VMEM((span, SUB, LANES), f32),
            pltpu.VMEM((tap_count, SUB, LANES), f32),
        ],
        name="lag_sum",
    )(lanes_first, taps)
    return jnp.concatenate([y[i] for i in range(width // LANES)], axis=1)


def split_lanes(x):
    return jnp.stack([x[:, i : i + LANES] for i in range(0, x.shape[1], LANES)], axis=0)


def join_lanes(x):
    return jnp.concatenate([x[i] for i in range(x.shape[0])], axis=1)


def mode_close(ahead, behind, rates):
    groups, rows, _ = ahead.shape
    modes, width = rates.shape
    length = rows // SUB
    unroll = 4

    def body(a_ref, b_ref, rate_ref, chunk_ref, shard_ref):
        order = lax.broadcasted_iota(jnp.int32, (SUB, LANES), 0).astype(f32)
        for way, src in enumerate((a_ref, b_ref)):
            for lane in range(groups):
                lanes = slice(lane * LANES, (lane + 1) * LANES)
                rate = [jnp.broadcast_to(rate_ref[m : m + 1, lanes], (SUB, LANES)) for m in range(modes)]
                decay = [jnp.exp(-r) for r in rate]

                def step(i, states):
                    states = list(states)
                    for u in range(unroll):
                        r = i * unroll + u
                        if way == 1:
                            r = length - 1 - r
                        x = src[lane, pl.ds(r, SUB, stride=length), :]
                        states = [decay[m] * states[m] + x for m in range(modes)]
                    return tuple(states)

                zero = tuple(jnp.zeros((SUB, LANES), f32) for _ in range(modes))
                states = lax.fori_loop(0, length // unroll, step, zero)
                after = (SUB - 1) - order if way == 0 else order
                for m in range(modes):
                    chunk_ref[way, m, :, lanes] = states[m]
                    weighted = states[m] * jnp.exp(-(rate[m] * (after * float(length))))
                    shard_ref[way, m : m + 1, lanes] = jnp.sum(weighted, axis=0, keepdims=True)

    vmem = pl.BlockSpec(memory_space=pltpu.VMEM)
    return pl.pallas_call(
        body,
        out_shape=[
            jax.ShapeDtypeStruct((2, modes, SUB, width), f32),
            jax.ShapeDtypeStruct((2, modes, width), f32),
        ],
        in_specs=[vmem] * 3,
        out_specs=[vmem] * 2,
        name="mode_close",
    )(ahead, behind, rates)


def mode_apply(ahead, behind, rates, residues, chunks, entering):
    groups, rows, _ = ahead.shape
    modes, _ = rates.shape
    length = rows // SUB
    unroll = 2

    def body(a_ref, b_ref, rate_ref, res_ref, chunk_ref, enter_ref, ya_ref, yb_ref):
        order = lax.broadcasted_iota(jnp.int32, (SUB, LANES), 0)
        for way, (src, dst) in enumerate(((a_ref, ya_ref), (b_ref, yb_ref))):
            place = order if way == 0 else (SUB - 1) - order
            for lane in range(groups):
                lanes = slice(lane * LANES, (lane + 1) * LANES)
                decay = []
                residue = []
                start = []
                for m in range(modes):
                    rate = jnp.broadcast_to(rate_ref[m : m + 1, lanes], (SUB, LANES))
                    decay.append(jnp.exp(-rate))
                    residue.append(jnp.broadcast_to(res_ref[m : m + 1, lanes], (SUB, LANES)))
                    first = jnp.broadcast_to(enter_ref[way, m : m + 1, lanes], (SUB, LANES))

                    def back(v, by):
                        moved = pltpu.roll(v, by if way == 0 else SUB - by, 0)
                        return moved

                    state = jnp.where(place == 0, first, back(chunk_ref[way, m, :, lanes], 1))
                    for by in (1, 2, 4):
                        factor = jnp.exp(-(rate * float(by * length)))
                        state = state + jnp.where(place >= by, factor * back(state, by), 0.0)
                    start.append(state)

                def step(i, states):
                    states = list(states)
                    for u in range(unroll):
                        r = i * unroll + u
                        if way == 1:
                            r = length - 1 - r
                        x = src[lane, pl.ds(r, SUB, stride=length), :]
                        states = [decay[m] * states[m] + x for m in range(modes)]
                        terms = [residue[m] * states[m] for m in range(modes)]
                        while len(terms) > 1:
                            terms = [a + b for a, b in zip(terms[::2], terms[1::2])]
                        dst[lane, pl.ds(r, SUB, stride=length), :] = terms[0]
                    return tuple(states)

                lax.fori_loop(0, length // unroll, step, tuple(start))

    vmem = pl.BlockSpec(memory_space=pltpu.VMEM)
    return pl.pallas_call(
        body,
        out_shape=[jax.ShapeDtypeStruct(ahead.shape, f32)] * 2,
        in_specs=[vmem] * 6,
        out_specs=[vmem] * 2,
        name="mode_apply",
    )(ahead, behind, rates, residues, chunks, entering)


def shift_axis(shard, axis, by):
    n = lax.axis_size(axis)
    pairs = [(i, i + by) for i in range(n) if 0 <= i + by < n]
    return lax.ppermute(shard, axis, pairs)


def taps_ahead(projected, short_filter, first, rows):
    tap_count = short_filter.shape[0]
    running = None
    for i in range(tap_count):
        term = short_filter[i] * projected[first - i : first - i + rows].astype(f32)
        running = term if running is None else running + term
    return running


def taps_behind(gradient, short_filter, rows):
    running = None
    for i in range(short_filter.shape[0]):
        term = short_filter[i] * gradient[i : i + rows].astype(f32)
        running = term if running is None else running + term
    return running


def normalise(whole, gain):
    as_float = whole.astype(f32)
    scale = lax.rsqrt(jnp.mean(as_float * as_float, axis=1) + epsilon)
    return (as_float * scale[:, None] * gain[None, :].astype(f32)).astype(bf16), scale


def last_ring_step(ring_sums, weight_part):
    at = lax.axis_index("seq")
    y, x_low = at // 2, lax.rem(at, 2)
    n_seq = lax.axis_size("seq")
    chip_rows = ring_sums.shape[1]
    arrived = [
        lax.ppermute(
            ring_sums[way], "seq", [(k, (k // 2 + step) % 4 * 2 + k % 2) for k in range(n_seq)]
        )
        for way, step in ((0, 1), (1, 3))
    ]
    own = lax.dynamic_slice_in_dim(weight_part, y * chip_rows, chip_rows, 0)
    sums = jnp.concatenate(arrived, axis=1).astype(f32) + own.astype(f32)
    part = chip_rows // 2
    theirs = lax.dynamic_slice_in_dim(sums, (1 - x_low) * part, part, 0).astype(bf16)
    return lax.dynamic_slice_in_dim(sums, x_low * part, part, 0), theirs


def cross(theirs):
    return lax.ppermute(theirs, "seq", [(k, k ^ 1) for k in range(lax.axis_size("seq"))]).astype(f32)


def small(vector):
    rows = vector.reshape(-1, LANES)
    pad = -rows.shape[0] % SUB
    return jnp.pad(rows, ((0, pad), (0, 0)))


def per_device(
    token_ids,
    embedding,
    gain_first,
    gain_second,
    weights_first,
    weights_second,
    short_first,
    short_second,
    medium,
    residues,
    decay_rates,
    cotangent,
):
    n_seq = lax.axis_size("seq")
    seq_at = lax.axis_index("seq")
    rows = token_ids.shape[0]
    vocab, width = embedding.shape
    features = weights_first.shape[0]
    wide = 3 * width
    vocab_part = vocab // n_seq
    flat_first = weights_first.reshape(features, wide)
    flat_second = weights_second.reshape(features, wide)
    taps_first = short_first.reshape(-1, wide)
    taps_second = short_second.reshape(-1, wide)

    packed = jnp.concatenate(
        [embedding, gain_first[None], gain_second[None], jnp.zeros((14, width), bf16)], axis=0
    )
    joined, around = ring_gather(0, "ch", packed, small(token_ids))
    before = jnp.where(seq_at == 0, -1, around[0].reshape(-1)[rows - HALO : rows])
    after = jnp.where(seq_at == n_seq - 1, -1, around[1].reshape(-1)[:HALO])
    ids = jnp.concatenate([before, token_ids, after])
    whole_gain_first, whole_gain_second = joined[vocab], joined[vocab + 1]
    table_normed, table_scale = normalise(joined[:vocab], whole_gain_first)
    table_projected = jnp.dot(table_normed, flat_first, preferred_element_type=f32).astype(bf16)
    table = jnp.concatenate([table_projected, embedding], axis=1)

    onehot = (ids[:, None] == jnp.arange(vocab, dtype=jnp.int32)[None, :]).astype(bf16)
    looked_up = jnp.dot(onehot, table, preferred_element_type=f32).astype(bf16)
    ahead = HALO - SUB
    featured_first = taps_ahead(looked_up[:, :wide], taps_first, SUB, looked_up.shape[0] - SUB)
    gated_first = (
        (featured_first[:, width : 2 * width] * featured_first[:, 2 * width :]).astype(bf16).astype(f32)
    )
    medium_float = medium.astype(f32)
    tap_count = medium.shape[0]
    out_rows = rows + 2 * LEAD
    begin = ahead - LEAD - (tap_count - 1)
    filtered_first = lag_sum(gated_first[begin : begin + out_rows + tap_count], medium_float)
    near = slice(ahead - LEAD, ahead - LEAD + out_rows)
    embedded = looked_up[HALO - LEAD : HALO - LEAD + out_rows, wide:].astype(f32)
    middle_near = (embedded + featured_first[near, :width] * filtered_first).astype(bf16)
    middle = middle_near[LEAD : LEAD + rows]

    whole_rows = ring_gather(1, "ch", middle_near)[0]
    normed_near, scale_near = normalise(whole_rows, whole_gain_second)
    normed_second, scale_second = normed_near[LEAD : LEAD + rows], scale_near[LEAD : LEAD + rows]
    projected_near = jnp.dot(normed_near, flat_second, preferred_element_type=f32).astype(bf16)
    featured_second = taps_ahead(projected_near, taps_second, LEAD, rows)
    pick = [featured_second[:, j * width : (j + 1) * width] for j in range(3)]
    gated_second = (pick[1] * pick[2]).astype(bf16).astype(f32)
    above_second = cotangent.astype(f32)
    grad_filtered = (above_second * pick[0]).astype(bf16).astype(f32)
    gated_lanes, grad_lanes = split_lanes(gated_second), split_lanes(grad_filtered)
    chunks, shard_states = mode_close(gated_lanes, grad_lanes, decay_rates)
    (all_states,) = exchange(2, [Item(shard_states, "seq", window="onward")])
    other = jnp.arange(n_seq, dtype=jnp.int32)
    gaps = jnp.stack([seq_at - 1 - other, other - 1 - seq_at], axis=1)
    all_states = all_states[:, None]
    weights_of = jnp.where(
        (gaps >= 0)[:, :, None, None],
        jnp.exp(-decay_rates[None, None] * (jnp.maximum(gaps, 0) * rows).astype(f32)[:, :, None, None]),
        0.0,
    )
    entering = jnp.sum(weights_of * all_states, axis=0)
    filtered_lanes, gated_grad_lanes = mode_apply(
        gated_lanes, grad_lanes, decay_rates, residues, chunks, entering
    )
    filtered_second, grad_gated = join_lanes(filtered_lanes), join_lanes(gated_grad_lanes)
    output = (middle.astype(f32) + pick[0] * filtered_second).astype(bf16)

    grad_featured = jnp.concatenate(
        [above_second * filtered_second, grad_gated * pick[2], grad_gated * pick[1]], axis=1
    ).astype(bf16)
    following = shift_axis(grad_featured[:SUB], "seq", -1)
    grad_projected = taps_behind(
        jnp.concatenate([grad_featured, following], axis=0), taps_second, rows
    ).astype(bf16)
    row_part = jnp.sum(
        grad_projected.astype(f32) * projected_near[LEAD : LEAD + rows].astype(f32), axis=1
    )
    partial_sum = lax.dot_general(
        grad_projected, flat_second, (((1,), (1,)), ((), ())), preferred_element_type=f32
    ).astype(bf16)
    weight_part = lax.dot_general(
        normed_second, grad_projected, (((0,), (0,)), ((), ())), preferred_element_type=f32
    ).astype(bf16)
    grad_normed, row_total, ring_sums = ring_scatter(3, "ch", partial_sum, small(row_part), weight_part)
    ours, theirs = last_ring_step(ring_sums, weight_part)
    row_total = row_total.reshape(-1)[:rows]
    middle_float = middle.astype(f32)
    scale = scale_second[:, None]
    grad_middle = (
        above_second
        + scale * grad_normed * gain_second.astype(f32)
        - middle_float * (scale * scale) * row_total[:, None] / features
    ).astype(bf16)
    gain_part_second = jnp.sum(grad_normed * middle_float * scale, axis=0)

    grad_near = jnp.concatenate([grad_middle, shift_axis(grad_middle[:HALO], "seq", -1)], axis=0)
    from_here = slice(ahead, ahead + rows + HALO)
    grad_filtered = (
        (grad_near.astype(f32) * featured_first[from_here, :width]).astype(bf16).astype(f32)
    )
    grad_gated = lag_sum(grad_filtered, medium_float[::-1])[: rows + SUB]
    here = slice(ahead, ahead + rows + SUB)
    grad_featured = jnp.concatenate(
        [
            grad_near[: rows + SUB].astype(f32) * filtered_first[LEAD:],
            grad_gated * featured_first[here, 2 * width :],
            grad_gated * featured_first[here, width : 2 * width],
        ],
        axis=1,
    ).astype(bf16)
    grad_projected = taps_behind(grad_featured, taps_first, rows).astype(bf16)
    by_token = lax.dot_general(
        onehot[HALO : HALO + rows],
        jnp.concatenate([grad_projected, grad_middle], axis=1),
        (((0,), (0,)), ((), ())),
        preferred_element_type=f32,
    ).astype(bf16)
    by_token, theirs = lax.optimization_barrier((by_token, theirs))
    crossed = cross(theirs)
    (token_sums,) = ring_scatter(4, "seq", by_token)
    weight_grad_second = ours + crossed
    token_grad = token_sums[:, :wide].astype(bf16)
    token_above = token_sums[:, wide:]
    own_part = lambda array: lax.dynamic_slice_in_dim(array, seq_at * vocab_part, vocab_part, 0)
    token_part = jnp.sum(token_grad.astype(f32) * own_part(table_projected).astype(f32), axis=1)
    token_partial = lax.dot_general(
        token_grad, flat_first, (((1,), (1,)), ((), ())), preferred_element_type=f32
    ).astype(bf16)
    token_normed, token_total = ring_scatter(5, "ch", token_partial, small(jnp.pad(token_part, (0, -vocab_part % LANES))))
    token_total = token_total.reshape(-1)[:vocab_part, None]
    table_float = own_part(embedding).astype(f32)
    scale = own_part(table_scale)[:, None]
    grad_table = (
        token_above
        + scale * token_normed * gain_first.astype(f32)
        - table_float * (scale * scale) * token_total / features
    )
    gain_part_first = jnp.sum(token_normed * table_float * scale, axis=0)
    highs = [part.astype(bf16) for part in (gain_part_first, gain_part_second)]
    lows = [
        (part - high.astype(f32)).astype(bf16)
        for part, high in zip((gain_part_first, gain_part_second), highs)
    ]
    gain_row = jnp.concatenate([highs[0], lows[0], highs[1], lows[1]])
    closing = jnp.concatenate(
        [
            jnp.concatenate([token_grad, grad_table.astype(bf16)], axis=1),
            gain_row[None],
            jnp.zeros((15, wide + width), bf16),
        ],
        axis=0,
    )
    (closed,) = ring_gather(6, "seq", closing)
    token_grads = closed[:, :vocab_part, :wide].reshape(vocab, wide)
    table_parts = closed[:, :vocab_part, wide:].reshape(vocab, width)
    gain_total = jnp.sum(closed[:, vocab_part].astype(f32).reshape(n_seq, 2, 2, width), axis=(0, 2))
    weight_grad_first = lax.dot_general(
        lax.dynamic_slice_in_dim(table_normed, seq_at * (features // n_seq), features // n_seq, 1),
        token_grads,
        (((0,), (0,)), ((), ())),
        preferred_element_type=f32,
    )
    return (
        output,
        table_parts.astype(f32),
        gain_total[0],
        gain_total[1],
        weight_grad_first.reshape(-1, 3, width),
        weight_grad_second.reshape(-1, 3, width),
    )


def solution(mesh):
    placed = (
        P("seq"),
        P(None, "ch"),
        P("ch"),
        P("ch"),
        P(None, None, "ch"),
        P(None, None, "ch"),
        P(None, None, "ch"),
        P(None, None, "ch"),
        P(None, "ch"),
        P(None, "ch"),
        P(None, "ch"),
        P("seq", "ch"),
    )
    return jax.shard_map(
        per_device,
        mesh=mesh,
        in_specs=placed,
        out_specs=(
            P("seq", "ch"),
            P(None, "ch"),
            P("ch"),
            P("ch"),
            P("seq", None, "ch"),
            P("seq", None, "ch"),
        ),
        check_vma=False,
    )
```
